512 devices in a mesh: seg: 16 (over y, core), band: 32 (over z, x).
Axes of the slice: x: 4, y: 8, z: 8, core: 2. Of those that a mesh axis runs over, the one named last changes fastest.
Arguments:
- sft: bfloat16 [32, 2, 2, 8192], P('seg', None, None, 'band'), may hold values from -6 to 6
- doppler: float32 [32, 512], P('seg'), may hold values from -16 to 16
- antenna: float32 [32, 2, 2, 512], P('seg'), may hold values from -1 to 1
- coarse_index: int32 [32, 512], P('seg'), may hold values from 0 to 511
- freq_offset: int32 [32, 512], P('seg'), may hold values from -32 to 32
- wing_width: int32 [32], replicated, may hold values from 8 to 32
Outputs:
- fstat: float32 [512, 8192], P('seg', 'band')
The draws below stay inside these ranges and needn't reach their ends.
All inputs are finite; a program needn't handle non-finite values.
Results may differ from the reference program's by a relative error of at most 0.00088.
Values may be sent and summed in bfloat16 or wider, within the bound.
No kernel may reach another device: no remote copies, remote signals or barrier semaphores. Data moves between devices by JAX's collectives and lax.ppermute only.
A program may use at most 64 MiB of HBM per device.

```python
import math
import jax
import jax.numpy as jnp
from jax import lax

DET = 2
WMAX = 32
OMAX = 32
BINS_DEV = 256
COARSE = 512
SEGMENTS = 32
BINS = 8192
FINE = 512
N_BAND = 32


def touch_ends(array, key, low, largest):
    dims = array.shape
    spot = [jax.random.randint(jax.random.fold_in(key, axis), (), 0, dims[axis]) for axis in range(len(dims))]
    array = array.at[tuple(spot)].set(low)
    longest = dims.index(max(dims))
    spot[longest] = (spot[longest] + 1) % dims[longest]
    return array.at[tuple(spot)].set(largest)


def block_levels(stream_key, shape, shards, least, high):
    def one(axis_at, parts):
        heights = jax.random.uniform(jax.random.fold_in(jax.random.fold_in(stream_key, 6), axis_at), (parts,), jnp.float32, least / len(shards), high / len(shards))
        return jnp.repeat(jnp.exp(heights), shape[axis_at] // parts).reshape((-1,) + (1,) * (len(shape) - axis_at - 1))

    loudness = one(*shards[0])
    for cut in shards[1:]:
        loudness = loudness * one(*cut)
    return loudness


def normal_values(stream_key, dims, scale, limit, pieces=(), held_as=jnp.bfloat16):
    entries = jax.random.normal(stream_key, dims, jnp.float32) * scale
    if len(pieces) > 0:
        entries = block_levels(stream_key, dims, pieces, -0.22, 0.18) * entries
    return jnp.clip(entries, min=-limit, max=limit).astype(held_as)


def setup_inputs(seed: int = 0) -> dict:
    key_of = jax.random.split(jax.random.key(seed), 7)
    return {
        "sft": normal_values(key_of[0], (SEGMENTS, DET, 2, BINS), 1.0, 6.0, ((0, 16), (3, 32))),
        "doppler": jnp.clip(jax.random.uniform(key_of[1], (SEGMENTS, COARSE), jnp.float32, -16.0, 16.0) * block_levels(key_of[1], (SEGMENTS, COARSE), ((0, 16),), -0.4, 0.0), -16.0, 16.0),
        "antenna": jnp.clip(jax.random.uniform(key_of[2], (SEGMENTS, 2, DET, COARSE), jnp.float32, -1.0, 1.0) * block_levels(key_of[2], (SEGMENTS, 2, DET, COARSE), ((0, 16),), -0.4, 0.0), -1.0, 1.0),
        "coarse_index": touch_ends(jax.random.randint(key_of[3], (SEGMENTS, FINE), 0, COARSE), jax.random.fold_in(key_of[3], 1), 0, COARSE - 1).astype(jnp.int32),
        "freq_offset": touch_ends(jax.random.randint(key_of[4], (SEGMENTS, FINE), 0 - OMAX, OMAX + 1), jax.random.fold_in(key_of[4], 1), 0 - OMAX, OMAX).astype(jnp.int32),
        "wing_width": touch_ends(jax.random.randint(key_of[5], (N_BAND,), WMAX // 4, WMAX + 1), jax.random.fold_in(key_of[5], 1), WMAX // 4, WMAX).astype(jnp.int32),
    }


def kernel_block(shifts, weights):
    tap_pos = jnp.arange(2 * WMAX).astype(jnp.float32) - WMAX
    offsets = tap_pos[None, None, :] - shifts[:, :, None]
    envelope = jnp.sinc(offsets)
    real_part = envelope * jnp.cos(jnp.pi * offsets)
    imag_part = -envelope * jnp.sin(jnp.pi * offsets)
    from_real = jnp.stack([real_part, imag_part], -1)
    from_imag = jnp.stack([-imag_part, real_part], -1)
    stacked = jnp.transpose(jnp.stack([from_real, from_imag], 1), (0, 1, 3, 2, 4))
    antenna_t = jnp.transpose(weights, (0, 2, 3, 1))
    product = antenna_t[:, :, None, None, :, :, None] * stacked[:, None, :, :, :, None, :]
    count_seg = shifts.shape[0]
    return product.astype(jnp.bfloat16).reshape(count_seg, -1, shifts.shape[1] * 4)


def coarse_stat(padded, doppler, antenna, wing_width, first_bin, bin_count, band_bins):
    segs_here = padded.shape[0]
    tap_count = 2 * WMAX
    unfolded = jnp.stack([padded[:, :, :, column:column + bin_count] for column in range(tap_count)], axis=3)
    global_bin = first_bin + jnp.arange(bin_count).astype(jnp.int32)
    subband = global_bin // band_bins
    member = subband[:, None] == jnp.arange(wing_width.shape[0]).astype(jnp.int32)[None, :]
    wing_reach = jnp.sum(jnp.where(member, wing_width[None, :], 0), axis=1)
    tap_index = jnp.arange(tap_count).astype(jnp.int32) - WMAX
    inside = (tap_index[:, None] >= -wing_reach[None, :]) & (tap_index[:, None] < wing_reach[None, :])
    unfolded = unfolded * inside.astype(jnp.bfloat16)
    unfolded = unfolded.reshape(segs_here, -1, bin_count).astype(jnp.float32)
    coarse_count = doppler.shape[1]
    block_size = math.gcd(coarse_count, 256)
    blocks = coarse_count // block_size
    shift_blocks = jnp.moveaxis(doppler.reshape(segs_here, blocks, block_size), 1, 0)
    weight_blocks = jnp.moveaxis(antenna.reshape(segs_here, 2, antenna.shape[2], blocks, block_size), 3, 0)

    def one_block(block_args):
        kernel = kernel_block(block_args[0], block_args[1]).astype(jnp.float32)
        amplitude = jnp.einsum("skf,skn->snf", unfolded, kernel)
        amplitude = amplitude.reshape(segs_here, block_size, 4, bin_count)
        return 0.25 * jnp.sum(amplitude * amplitude, axis=2)

    result = lax.map(one_block, (shift_blocks, weight_blocks))
    return jnp.transpose(result, (1, 0, 2, 3)).reshape(segs_here, coarse_count, bin_count)


def reference(sft, doppler, antenna, coarse_index, freq_offset, wing_width):
    all_bins = sft.shape[3]

    def one_segment(partial_sum, inputs):
        segment_sft, shifts, weights, indices, offsets = inputs
        padded = jnp.pad(segment_sft, ((0, 0), (0, 0), (WMAX, WMAX)))[None]
        coarse = coarse_stat(padded, shifts[None], weights[None], wing_width, 0, all_bins, BINS_DEV)[0]
        coarse = jnp.pad(coarse, ((0, 0), (OMAX, OMAX)))
        picked = jnp.take(coarse, indices, axis=0)
        moved = jax.vmap(lambda row_data, shift_bins: lax.dynamic_slice_in_dim(row_data, (shift_bins + OMAX).astype(jnp.int32), all_bins))(picked, offsets)
        return partial_sum + moved, None

    initial = jnp.zeros((coarse_index.shape[1], all_bins), jnp.float32)
    total, unused = lax.scan(one_segment, initial, (sft, doppler, antenna, coarse_index, freq_offset))
    return total / SEGMENTS
```

```python
import functools

import jax
import jax.numpy as jnp
from jax import lax
from jax.experimental import pallas as pl
from jax.experimental.pallas import tpu as pltpu
from jax.sharding import PartitionSpec as P

WMAX = 32
OMAX = 32
LANES = 128
HALO = WMAX + OMAX
SFT_ROWS = 24
PARAM_ROWS = 16
ROWS = SFT_ROWS + PARAM_ROWS
VMEM = pltpu.VMEM
F32 = jnp.float32
BF16 = jnp.bfloat16


def pieces(value):
    high = value.astype(BF16)
    rest = value - high.astype(F32)
    middle = rest.astype(BF16)
    low = (rest - middle.astype(F32)).astype(BF16)
    return high, middle, low


def lane_iota(shape):
    return lax.broadcasted_iota(jnp.int32, shape, len(shape) - 1)


def row_iota(shape):
    return lax.broadcasted_iota(jnp.int32, shape, len(shape) - 2)


def choose_params(doppler_ref, antenna_ref, index_ref, offset_ref, out_ref):
    coarse = doppler_ref.shape[1]
    fine = index_ref.shape[1]
    own = fine // out_ref.shape[0]
    per_tile = LANES // own
    lanes = lane_iota((PARAM_ROWS, LANES))
    tiles = []
    for seg in range(2):
        values = jnp.concatenate(
            [doppler_ref[seg : seg + 1, :]]
            + [antenna_ref[seg, q, d : d + 1, :] for q in range(2) for d in range(2)], 0
        )
        high, middle, low = pieces(values)
        table = jnp.concatenate(
            [high.astype(F32), middle.astype(F32), low.astype(F32), jnp.zeros((1, coarse), F32)], 0
        ).astype(BF16)
        hot = row_iota((coarse, fine)) == index_ref[seg : seg + 1, :]
        chosen = jnp.dot(table, jnp.where(hot, 1.0, 0.0).astype(BF16), preferred_element_type=F32)
        shift = jnp.broadcast_to(offset_ref[seg : seg + 1, :].astype(F32), chosen.shape)
        chosen = jnp.where(row_iota(chosen.shape) == PARAM_ROWS - 1, shift, chosen)
        tiles.append(chosen)
    for peer in range(out_ref.shape[0]):
        tile, place = divmod(peer, per_tile)
        cols = slice(tile * LANES, (tile + 1) * LANES)
        first = pltpu.roll(tiles[0][:, cols], (LANES - place * own) % LANES, 1)
        second = pltpu.roll(tiles[1][:, cols], (LANES - place * own + own) % LANES, 1)
        out_ref[peer] = jnp.where(lanes < own, first, second).astype(BF16)


def pack(left_ref, own_ref, right_ref, params_ref, out_ref):
    bins = own_ref.shape[3]
    rows = []
    for ref, start in ((left_ref, bins - HALO), (own_ref, 0), (right_ref, 0)):
        width = bins if ref is own_ref else HALO
        rows.append(jnp.concatenate(
            [ref[s, d, :, start : start + width].astype(F32) for s in range(2) for d in range(2)], 0
        ))
    padded = jnp.concatenate(rows, 1)
    mirror = jnp.where(
        row_iota((LANES, LANES)) + lane_iota((LANES, LANES)) == LANES - 1, 1.0, 0.0
    ).astype(BF16)
    chunks = jnp.concatenate(
        [padded[:, c * LANES : (c + 1) * LANES] for c in reversed(range(SFT_ROWS // 8))], 0
    ).astype(BF16)
    block = jnp.dot(chunks, mirror, preferred_element_type=F32).astype(BF16)
    for peer in range(out_ref.shape[0]):
        out_ref[peer, :SFT_ROWS, :] = block
        out_ref[peer, SFT_ROWS:, :] = params_ref[peer]


def fine_stat(scale, wing_ref, recv_ref, out_ref, x_ref, m_ref, edge_ref, t_ref, k_ref, acc_ref):
    peers = recv_ref.shape[0]
    fine, bins = out_ref.shape
    band = lax.axis_index("band")
    last = lax.axis_size("band") - 1
    w_own = wing_ref[band].astype(F32)
    w_prev = jnp.where(band > 0, wing_ref[jnp.maximum(band - 1, 0)], 0).astype(F32)
    w_next = jnp.where(band < last, wing_ref[jnp.minimum(band + 1, last)], 0).astype(F32)

    lanes16 = lane_iota((peers, LANES))
    part = lambda i: recv_ref[:, SFT_ROWS + i, :].astype(F32)
    whole = lambda i: part(i) + part(5 + i) + part(10 + i)
    doppler = whole(0)
    shift = part(PARAM_ROWS - 1)
    frac = doppler - jnp.round(doppler)
    factor = jnp.sin(jnp.pi * frac) * (1.0 / jnp.pi)
    wing = jnp.where(shift < 0, w_prev, w_next)
    for i, row in enumerate([doppler, shift, factor, wing, whole(1), whole(2), whole(3), whole(4)]):
        m_ref[:, i, :] = row
    for seg in range(2):
        group = jnp.where(lanes16 // fine == seg, shift, 0.0)
        group = group + pltpu.roll(group, 2 * fine, 1)
        group = group + pltpu.roll(group, fine, 1)
        edge_ref[:, seg, :] = group
    acc_ref[...] = jnp.zeros_like(acc_ref)

    tap = (HALO - 1) - lane_iota((fine, LANES)).astype(F32)
    bend = lane_iota((16, LANES)) - row_iota((16, LANES))
    lane = lane_iota((OMAX, LANES))
    row = row_iota((OMAX, LANES)).astype(F32)
    other = lane >= LANES // 2

    @pl.loop(0, peers)
    def _(peer):
        x_ref[...] = recv_ref[peer, :SFT_ROWS, :].astype(F32)
        columns = m_ref[peer].T
        for seg in range(2):
            here = columns[seg * fine : (seg + 1) * fine, :]
            col = lambda i: jnp.broadcast_to(here[:, i : i + 1], (fine, LANES))
            offset = col(1)
            k = tap - offset
            u = k - col(0)
            envelope = jnp.where(u == 0, 1.0, col(2) / jnp.where(u == 0, 1.0, u))
            middle = jnp.abs(k + 0.5)
            for v, width in ((0, w_own), (1, col(3))):
                masked = jnp.where(middle < width, envelope, 0.0)
                for q in range(2):
                    for d in range(2):
                        at = (v * 2 + q) * fine
                        k_ref[seg, at : at + fine, d * LANES : (d + 1) * LANES] = (
                            masked * col(4 + q * 2 + d)
                        ).astype(BF16)
            for d in range(2):
                for ri in range(2):
                    at = seg * 4 + d * 2 + ri
                    spread = [
                        jnp.broadcast_to(x_ref[c * 8 + at : c * 8 + at + 1, :], (16, LANES))
                        for c in range(SFT_ROWS // 8)
                    ]
                    for a in range(1, LANES // 16 + 1):
                        turned = [
                            pltpu.roll(s, LANES - 16 * a, 1, stride=1, stride_axis=0)
                            for s in spread
                        ]
                        inside = bend < LANES - 16 * a
                        for c in range(bins // LANES):
                            start = (ri + 1) * bins - c * LANES - 16 * a
                            t_ref[seg, start : start + 16, d * LANES : (d + 1) * LANES] = jnp.where(
                                inside, turned[c], turned[c + 1]
                            ).astype(BF16)
            amp = lax.dot_general(
                t_ref[seg], k_ref[seg], (((1,), (1,)), ((), ())), preferred_element_type=F32
            )
            power = amp[:bins] * amp[:bins] + amp[bins:] * amp[bins:]
            edge = edge_ref[peer, seg : seg + 1, :]
            low_ok = (row >= -edge) != other
            high_ok = (row < OMAX - edge) != other
            acc_ref[:OMAX, :] += jnp.where(low_ok, power[:OMAX], 0.0)
            acc_ref[OMAX : bins - OMAX, :] += power[OMAX : bins - OMAX]
            acc_ref[bins - OMAX :, :] += jnp.where(high_ok, power[bins - OMAX :], 0.0)

    f = row_iota((bins, LANES))
    keep = (lane_iota((bins, LANES)) < LANES // 2) | (f < OMAX) | (f >= bins - OMAX)
    total = jnp.where(keep, acc_ref[...], 0.0)
    total = total + pltpu.roll(total, LANES // 2, 1)
    total = total + pltpu.roll(total, LANES // 4, 1)
    out_ref[...] = total.T[:fine, :] * scale


def per_device(sft, doppler, antenna, coarse_index, freq_offset, wing_width):
    bins = sft.shape[3]
    peers = lax.axis_size("seg")
    count = lax.axis_size("band")
    fine = coarse_index.shape[1] // peers
    segments = sft.shape[0] * peers
    up = [(i, i + 1) for i in range(count - 1)]
    left = lax.ppermute(sft, "band", up)
    right = lax.ppermute(sft, "band", [(b, a) for a, b in up])
    params = pl.pallas_call(
        choose_params,
        out_shape=jax.ShapeDtypeStruct((peers, PARAM_ROWS, LANES), BF16),
        name="choose_params",
    )(doppler, antenna, coarse_index, freq_offset)
    sent = pl.pallas_call(
        pack, out_shape=jax.ShapeDtypeStruct((peers, ROWS, LANES), BF16), name="pack"
    )(left, sft, right, params)
    recv = lax.all_to_all(sent, "seg", 0, 0, tiled=True)
    return fine_call(recv, wing_width, fine, bins, peers, segments)


def fine_call(recv, wing_width, fine, bins, peers, segments):
    return pl.pallas_call(
        functools.partial(fine_stat, 1.0 / (4 * segments)),
        out_shape=jax.ShapeDtypeStruct((fine, bins), F32),
        in_specs=[pl.BlockSpec(memory_space=pltpu.SMEM), pl.BlockSpec(memory_space=VMEM)],
        scratch_shapes=[
            VMEM((SFT_ROWS, LANES), F32),
            VMEM((peers, 8, LANES), F32),
            VMEM((peers, 2, LANES), F32),
            VMEM((2, 2 * bins, 2 * LANES), BF16),
            VMEM((2, 4 * fine, 2 * LANES), BF16),
            VMEM((bins, LANES), F32),
        ],
        name="fine_stat",
    )(wing_width, recv)


def solution(mesh):
    placed = (
        P("seg", None, None, "band"),
        P("seg", None),
        P("seg", None, None, None),
        P("seg", None),
        P("seg", None),
        P(),
    )
    return jax.shard_map(
        per_device, mesh=mesh, in_specs=placed, out_specs=P("seg", "band"), check_vma=False
    )
```

```python
import math

import jax
import jax.numpy as jnp
from jax import lax
from jax.experimental import pallas as pl
from jax.experimental.pallas import tpu as pltpu
from jax.sharding import PartitionSpec as P

WMAX = 32
OMAX = 32
LANES = 128
TAPS = 2 * WMAX
HALF = LANES // 2
VMEM = pltpu.VMEM
F32 = jnp.float32
BF16 = jnp.bfloat16


def lane_iota(shape):
    return lax.broadcasted_iota(jnp.int32, shape, len(shape) - 1)


def row_iota(shape):
    return lax.broadcasted_iota(jnp.int32, shape, len(shape) - 2)


def split(value, count):
    parts = []
    for _ in range(count):
        part = value.astype(BF16)
        parts.append(part)
        value = value - part.astype(F32)
    return parts


def sin_pi_over_pi(r):
    r2 = r * r
    total = jnp.zeros_like(r)
    for n in reversed(range(8)):
        total = total * r2 + (-1) ** n * math.pi ** (2 * n) / math.factorial(2 * n + 1)
    return total * r


def make_taps(doppler_ref, antenna_ref, index_ref, out_ref):
    coarse = doppler_ref.shape[1]
    fine = index_ref.shape[1]
    tap = (WMAX - 1) - row_iota((TAPS, LANES)).astype(F32)
    for seg in range(2):
        values = jnp.concatenate(
            [doppler_ref[seg : seg + 1, :]]
            + [antenna_ref[seg, q, d : d + 1, :] for q in range(2) for d in range(2)], 0
        )
        table = jnp.concatenate(
            [part.astype(F32) for part in split(values, 3)] + [jnp.zeros((1, coarse), F32)], 0
        ).astype(BF16)
        for tile in range(fine // LANES):
            cols = slice(tile * LANES, (tile + 1) * LANES)
            hot = row_iota((coarse, LANES)) == index_ref[seg : seg + 1, cols]
            chosen = jnp.dot(table, jnp.where(hot, 1.0, 0.0).astype(BF16), preferred_element_type=F32)
            whole = chosen[0:5] + chosen[5:10] + chosen[10:15]
            shift = whole[0:1]
            factor = sin_pi_over_pi(shift - jnp.round(shift))
            u = tap - shift
            envelope = jnp.where(u == 0, 1.0, factor / u)
            for q in range(2):
                at = (tile * 2 + q) * LANES
                for d in range(2):
                    high, low = split(envelope * whole[1 + q * 2 + d : 2 + q * 2 + d], 2)
                    out_ref[seg, d * TAPS : (d + 1) * TAPS, at : at + LANES] = high
                    out_ref[seg, (2 + d) * TAPS : (3 + d) * TAPS, at : at + LANES] = low


def segment_sums(
    wing_ref, offset_ref, left_ref, own_ref, right_ref, taps_ref, out_ref,
    chunk_ref, t_ref, p_ref, u_ref, v_ref, acc_ref
):
    bins = own_ref.shape[3]
    span = bins + 2 * OMAX
    blocks = span // 16
    band = lax.axis_index("band")
    last = lax.axis_size("band") - 1
    w_own = wing_ref[band].astype(F32)
    w_prev = jnp.where(band > 0, wing_ref[jnp.maximum(band - 1, 0)], 0).astype(F32)
    w_next = jnp.where(band < last, wing_ref[jnp.minimum(band + 1, last)], 0).astype(F32)

    mirror = jnp.where(
        row_iota((LANES, LANES)) + lane_iota((LANES, LANES)) == LANES - 1, 1.0, 0.0
    ).astype(BF16)

    def rows_of(ref, start):
        return jnp.concatenate(
            [ref[s, d, :, start : start + LANES].astype(F32) for s in range(2) for d in range(2)], 0
        )

    parts = [rows_of(right_ref, 0)]
    parts += [rows_of(own_ref, c * LANES) for c in reversed(range(bins // LANES))]
    parts += [rows_of(left_ref, bins - LANES)]
    flipped = jnp.dot(
        jnp.concatenate(parts, 0).astype(BF16), mirror, preferred_element_type=F32
    )
    swapped = pltpu.roll(flipped, HALF, 1)
    for i in range(len(parts)):
        chunk_ref[0, i] = flipped[8 * i : 8 * i + 8]
        chunk_ref[1, i] = swapped[8 * i : 8 * i + 8]

    lane = lane_iota((16, LANES))
    low_half = lane < HALF
    within = lane % HALF
    bend = within - row_iota((16, LANES))
    center = jnp.abs((WMAX - 0.5) - within.astype(F32))
    reach = [center < w for w in (w_prev, w_own, w_next)]

    def half_row(h, place, row):
        chunk, half = (h + 1) // 2, (h + 1) % 2
        return jnp.broadcast_to(chunk_ref[half ^ place, chunk, row : row + 1, :], (16, LANES))

    def build(seg):
        for ri in range(2):
            first, second = seg * 4 + ri, seg * 4 + 2 + ri
            halves = span // HALF
            for h in range(halves):
                source = jnp.where(low_half, half_row(h, 0, first), half_row(h, 1, second))
                after = jnp.where(low_half, half_row(h + 1, 0, second), half_row(h + 1, 1, first))
                for a in range(1, 5):
                    turn = LANES - 16 * a
                    window = jnp.where(
                        bend < HALF - 16 * a,
                        pltpu.roll(source, turn, 1, stride=1, stride_axis=0),
                        pltpu.roll(after, turn, 1, stride=1, stride_axis=0),
                    )
                    block = blocks - 4 * h - a
                    side = 0 if block < OMAX // 16 else (2 if block >= blocks - OMAX // 16 else 1)
                    window = jnp.where(reach[side], window, 0.0).astype(BF16)
                    start = block * 32 + ri * 16
                    t_ref[seg, start : start + 16, :LANES] = window
                    t_ref[seg, start : start + 16, LANES:] = window

    def moved(seg, tile, slot):
        amount = offset_ref[seg : seg + 1, tile * LANES : (tile + 1) * LANES] + OMAX
        bit = lambda b: jnp.broadcast_to((amount & b) != 0, (8, LANES))
        size = bins // 8
        tiles = [p_ref[slot, 8 * t : 8 * t + 8, :] for t in range(span // 8)]
        far = bit(64)
        tiles = [jnp.where(far, tiles[t + 8], tiles[t]) for t in range(size)] + tiles[size:]
        for b in (32, 16, 8):
            pick, step = bit(b), b // 8
            tiles = [jnp.where(pick, tiles[t + step], tiles[t]) for t in range(size + step)]
        for t, value in enumerate(tiles):
            u_ref[slot, 8 * t : 8 * t + 8, :] = value
        pick = bit(4)
        for t in range(size + 1):
            end = min(8, bins + 4 - 8 * t)
            v_ref[slot, 8 * t : 8 * t + end, :] = jnp.where(
                pick[:end], u_ref[slot, 8 * t + 4 : 8 * t + 4 + end, :], u_ref[slot, 8 * t : 8 * t + end, :]
            )
        pick = bit(2)
        for t in range(size + 1):
            end = min(8, bins + 2 - 8 * t)
            u_ref[slot, 8 * t : 8 * t + end, :] = jnp.where(
                pick[:end], v_ref[slot, 8 * t + 2 : 8 * t + 2 + end, :], v_ref[slot, 8 * t : 8 * t + end, :]
            )
        pick = bit(1)
        return [
            jnp.where(pick, u_ref[slot, 8 * t + 1 : 8 * t + 9, :], u_ref[slot, 8 * t : 8 * t + 8, :])
            for t in range(size)
        ]

    tiles = offset_ref.shape[1] // LANES
    build(0)
    for seg in range(2):
        if seg == 0:
            build(1)
        for tile in range(tiles):
            slot = seg * tiles + tile
            amp = jnp.dot(
                t_ref[seg], taps_ref[seg, :, tile * 2 * LANES : (tile + 1) * 2 * LANES],
                preferred_element_type=F32,
            )
            power = (amp * amp).reshape(blocks, 2, 16, 2 * LANES).sum(axis=1)
            power = power.reshape(span, 2 * LANES)
            p_ref[slot] = power[:, :LANES] + power[:, LANES:]
            for t, value in enumerate(moved(seg, tile, slot)):
                if seg == 0:
                    acc_ref[tile, 8 * t : 8 * t + 8, :] = value
                else:
                    acc_ref[tile, 8 * t : 8 * t + 8, :] += value
    each = LANES // out_ref.shape[1]
    for tile in range(tiles):
        turned = acc_ref[tile].T.astype(BF16)
        out_ref[tile * each : (tile + 1) * each] = turned.reshape(each, LANES // each, bins)


def total(scale, recv_ref, out_ref):
    value = recv_ref[0].astype(F32)
    for peer in range(1, recv_ref.shape[0]):
        value = value + recv_ref[peer].astype(F32)
    out_ref[...] = value * scale


def per_device(sft, doppler, antenna, coarse_index, freq_offset, wing_width):
    bins = sft.shape[3]
    peers = lax.axis_size("seg")
    count = lax.axis_size("band")
    templates = coarse_index.shape[1]
    fine = templates // peers
    segments = sft.shape[0] * peers
    tiles = templates // LANES
    span = bins + 2 * OMAX
    up = [(i, i + 1) for i in range(count - 1)]
    left = lax.ppermute(sft, "band", up)
    right = lax.ppermute(sft, "band", [(b, a) for a, b in up])
    taps = pl.pallas_call(
        make_taps,
        out_shape=jax.ShapeDtypeStruct((2, 4 * TAPS, 2 * templates), BF16),
        name="make_taps",
    )(doppler, antenna, coarse_index)
    vmem = pl.BlockSpec(memory_space=VMEM)
    sent = pl.pallas_call(
        segment_sums,
        out_shape=jax.ShapeDtypeStruct((peers, fine, bins), BF16),
        in_specs=[pl.BlockSpec(memory_space=pltpu.SMEM)] + [vmem] * 5,
        scratch_shapes=[
            VMEM((2, bins // LANES + 2, 8, LANES), F32),
            VMEM((2, 2 * span, 2 * LANES), BF16),
            VMEM((2 * tiles, span, LANES), F32),
            VMEM((2 * tiles, bins + 8, LANES), F32),
            VMEM((2 * tiles, bins + 8, LANES), F32),
            VMEM((tiles, bins, LANES), F32),
        ],
        name="segment_sums",
    )(wing_width, freq_offset, left, sft, right, taps)
    recv = lax.all_to_all(sent, "seg", 0, 0, tiled=True)
    return pl.pallas_call(
        lambda *refs: total(1.0 / (4 * segments), *refs),
        out_shape=jax.ShapeDtypeStruct((fine, bins), F32),
        name="total",
    )(recv)


def solution(mesh):
    placed = (
        P("seg", None, None, "band"),
        P("seg", None),
        P("seg", None, None, None),
        P("seg", None),
        P("seg", None),
        P(),
    )
    return jax.shard_map(
        per_device, mesh=mesh, in_specs=placed, out_specs=P("seg", "band"), check_vma=False
    )
```

```python
import functools
import math

import jax
import jax.numpy as jnp
from jax import lax
from jax.experimental import pallas as pl
from jax.experimental.pallas import tpu as pltpu
from jax.sharding import PartitionSpec as P

WMAX = 32
OMAX = 32
LANES = 128
TAPS = 2 * WMAX
HALF = LANES // 2
VMEM = pltpu.VMEM
F32 = jnp.float32
BF16 = jnp.bfloat16


def lane_iota(shape):
    return lax.broadcasted_iota(jnp.int32, shape, len(shape) - 1)


def row_iota(shape):
    return lax.broadcasted_iota(jnp.int32, shape, len(shape) - 2)


def split(value, count):
    parts = []
    for _ in range(count):
        part = value.astype(BF16)
        parts.append(part)
        value = value - part.astype(F32)
    return parts


def sin_pi_over_pi(r):
    r2 = r * r
    total = jnp.zeros_like(r)
    for n in reversed(range(8)):
        total = total * r2 + (-1) ** n * math.pi ** (2 * n) / math.factorial(2 * n + 1)
    return total * r


def near(value):
    return pltpu.with_memory_space_constraint(value, VMEM)


def make_taps(doppler_ref, antenna_ref, index_ref, out_ref):
    coarse = doppler_ref.shape[1]
    fine = index_ref.shape[1]
    tap = (WMAX - 1) - row_iota((TAPS, LANES)).astype(F32)
    for seg in range(2):
        values = jnp.concatenate(
            [doppler_ref[seg : seg + 1, :]]
            + [antenna_ref[seg, q, d : d + 1, :] for q in range(2) for d in range(2)], 0
        )
        table = jnp.concatenate(
            [part.astype(F32) for part in split(values, 3)] + [jnp.zeros((1, coarse), F32)], 0
        ).astype(BF16)
        for tile in range(fine // LANES):
            cols = slice(tile * LANES, (tile + 1) * LANES)
            hot = row_iota((coarse, LANES)) == index_ref[seg : seg + 1, cols]
            chosen = jnp.dot(table, jnp.where(hot, 1.0, 0.0).astype(BF16), preferred_element_type=F32)
            whole = chosen[0:5] + chosen[5:10] + chosen[10:15]
            shift = whole[0:1]
            factor = sin_pi_over_pi(shift - jnp.round(shift))
            u = tap - shift
            envelope = jnp.where(u == 0, 1.0, factor / u)
            for q in range(2):
                at = (tile * 2 + q) * LANES
                for d in range(2):
                    high, low = split(envelope * whole[1 + q * 2 + d : 2 + q * 2 + d], 2)
                    out_ref[seg, d * TAPS : (d + 1) * TAPS, at : at + LANES] = high
                    out_ref[seg, (2 + d) * TAPS : (3 + d) * TAPS, at : at + LANES] = low


def segment_sums(
    scale, wing_ref, offset_ref, left_ref, own_ref, right_ref, taps_ref, out_ref,
    chunk_ref, t_ref, p_ref, u_ref, v_ref, acc_ref
):
    bins = own_ref.shape[3]
    span = bins + 2 * OMAX
    blocks = span // 16
    band = lax.axis_index("band")
    last = lax.axis_size("band") - 1
    w_own = wing_ref[band].astype(F32)
    w_prev = jnp.where(band > 0, wing_ref[jnp.maximum(band - 1, 0)], 0).astype(F32)
    w_next = jnp.where(band < last, wing_ref[jnp.minimum(band + 1, last)], 0).astype(F32)

    mirror = jnp.where(
        row_iota((LANES, LANES)) + lane_iota((LANES, LANES)) == LANES - 1, 1.0, 0.0
    ).astype(BF16)

    def rows_of(ref, start):
        return jnp.concatenate(
            [ref[s, d, :, start : start + LANES].astype(F32) for s in range(2) for d in range(2)], 0
        )

    parts = [rows_of(right_ref, 0)]
    parts += [rows_of(own_ref, c * LANES) for c in reversed(range(bins // LANES))]
    parts += [rows_of(left_ref, bins - LANES)]
    flipped = jnp.dot(
        jnp.concatenate(parts, 0).astype(BF16), mirror, preferred_element_type=F32
    )
    swapped = pltpu.roll(flipped, HALF, 1)
    for i in range(len(parts)):
        chunk_ref[0, i] = flipped[8 * i : 8 * i + 8]
        chunk_ref[1, i] = swapped[8 * i : 8 * i + 8]

    lane = lane_iota((16, LANES))
    low_half = lane < HALF
    within = lane % HALF
    bend = within - row_iota((16, LANES))
    center = jnp.abs((WMAX - 0.5) - within.astype(F32))
    reach = [center < w for w in (w_prev, w_own, w_next)]

    def half_row(h, place, row):
        chunk, half = (h + 1) // 2, (h + 1) % 2
        return jnp.broadcast_to(chunk_ref[half ^ place, chunk, row : row + 1, :], (16, LANES))

    def build(seg):
        for ri in range(2):
            first, second = seg * 4 + ri, seg * 4 + 2 + ri
            halves = span // HALF
            for h in range(halves):
                source = jnp.where(low_half, half_row(h, 0, first), half_row(h, 1, second))
                after = jnp.where(low_half, half_row(h + 1, 0, second), half_row(h + 1, 1, first))
                for a in range(1, 5):
                    turn = LANES - 16 * a
                    window = jnp.where(
                        bend < HALF - 16 * a,
                        pltpu.roll(source, turn, 1, stride=1, stride_axis=0),
                        pltpu.roll(after, turn, 1, stride=1, stride_axis=0),
                    )
                    block = blocks - 4 * h - a
                    side = 0 if block < OMAX // 16 else (2 if block >= blocks - OMAX // 16 else 1)
                    window = jnp.where(reach[side], window, 0.0).astype(BF16)
                    start = block * 32 + ri * 16
                    t_ref[seg, start : start + 16, :LANES] = window
                    t_ref[seg, start : start + 16, LANES:] = window

    def moved(seg, tile, slot):
        amount = offset_ref[seg : seg + 1, tile * LANES : (tile + 1) * LANES] + OMAX
        bit = lambda b: jnp.broadcast_to((amount & b) != 0, (8, LANES))
        size = bins // 8
        tiles = [p_ref[slot, 8 * t : 8 * t + 8, :] for t in range(span // 8)]
        far = bit(64)
        tiles = [jnp.where(far, tiles[t + 8], tiles[t]) for t in range(size)] + tiles[size:]
        for b in (32, 16, 8):
            pick, step = bit(b), b // 8
            tiles = [jnp.where(pick, tiles[t + step], tiles[t]) for t in range(size + step)]
        for t, value in enumerate(tiles):
            u_ref[slot, 8 * t : 8 * t + 8, :] = value
        pick = bit(4)
        for t in range(size + 1):
            end = min(8, bins + 4 - 8 * t)
            v_ref[slot, 8 * t : 8 * t + end, :] = jnp.where(
                pick[:end], u_ref[slot, 8 * t + 4 : 8 * t + 4 + end, :], u_ref[slot, 8 * t : 8 * t + end, :]
            )
        pick = bit(2)
        for t in range(size + 1):
            end = min(8, bins + 2 - 8 * t)
            u_ref[slot, 8 * t : 8 * t + end, :] = jnp.where(
                pick[:end], v_ref[slot, 8 * t + 2 : 8 * t + 2 + end, :], v_ref[slot, 8 * t : 8 * t + end, :]
            )
        pick = bit(1)
        return [
            jnp.where(pick, u_ref[slot, 8 * t + 1 : 8 * t + 9, :], u_ref[slot, 8 * t : 8 * t + 8, :])
            for t in range(size)
        ]

    tiles = offset_ref.shape[1] // LANES
    build(0)
    for seg in range(2):
        if seg == 0:
            build(1)
        for tile in range(tiles):
            slot = seg * tiles + tile
            amp = jnp.dot(
                t_ref[seg], taps_ref[seg, :, tile * 2 * LANES : (tile + 1) * 2 * LANES],
                preferred_element_type=F32,
            )
            power = (amp * amp).reshape(blocks, 2, 16, 2 * LANES).sum(axis=1)
            power = power.reshape(span, 2 * LANES)
            p_ref[slot] = power[:, :LANES] + power[:, LANES:]
            for t, value in enumerate(moved(seg, tile, slot)):
                if seg == 0:
                    acc_ref[tile, 8 * t : 8 * t + 8, :] = value
                else:
                    acc_ref[tile, 8 * t : 8 * t + 8, :] += value
    each = LANES // out_ref.shape[1]
    for tile in range(tiles):
        turned = (acc_ref[tile] * scale).T.astype(BF16)
        out_ref[tile * each : (tile + 1) * each] = turned.reshape(each, LANES // each, bins)


def per_device(sft, doppler, antenna, coarse_index, freq_offset, wing_width):
    bins = sft.shape[3]
    peers = lax.axis_size("seg")
    count = lax.axis_size("band")
    templates = coarse_index.shape[1]
    fine = templates // peers
    segments = sft.shape[0] * peers
    tiles = templates // LANES
    span = bins + 2 * OMAX
    up = [(i, i + 1) for i in range(count - 1)]
    left = lax.ppermute(sft, "band", up)
    right = lax.ppermute(sft, "band", [(b, a) for a, b in up])
    taps = pl.pallas_call(
        make_taps,
        out_shape=VMEM((2, 4 * TAPS, 2 * templates), BF16),
        name="make_taps",
    )(near(doppler), near(antenna), near(coarse_index))
    vmem = pl.BlockSpec(memory_space=VMEM)
    sent = pl.pallas_call(
        functools.partial(segment_sums, 1.0 / (4 * segments)),
        out_shape=VMEM((peers, fine, bins), BF16),
        in_specs=[pl.BlockSpec(memory_space=pltpu.SMEM)] + [vmem] * 5,
        scratch_shapes=[
            VMEM((2, bins // LANES + 2, 8, LANES), F32),
            VMEM((2, 2 * span, 2 * LANES), BF16),
            VMEM((2 * tiles, span, LANES), F32),
            VMEM((2 * tiles, bins + 8, LANES), F32),
            VMEM((2 * tiles, bins + 8, LANES), F32),
            VMEM((tiles, bins, LANES), F32),
        ],
        name="segment_sums",
    )(wing_width, *[near(z) for z in (freq_offset, left, sft, right, taps)])
    recv = lax.all_to_all(sent, "seg", 0, 0, tiled=True)
    return jnp.sum(recv.astype(F32), 0)


def solution(mesh):
    placed = (
        P("seg", None, None, "band"),
        P("seg", None),
        P("seg", None, None, None),
        P("seg", None),
        P("seg", None),
        P(),
    )
    return jax.shard_map(
        per_device, mesh=mesh, in_specs=placed, out_specs=P("seg", "band"), check_vma=False
    )
```

```python
import functools
import math

import jax
import jax.numpy as jnp
from jax import lax
from jax.experimental import pallas as pl
from jax.experimental.pallas import tpu as pltpu
from jax.sharding import PartitionSpec as P

WMAX = 32
OMAX = 32
LANES = 128
TAPS = 2 * WMAX
HALF = LANES // 2
VMEM = pltpu.VMEM
F32 = jnp.float32
BF16 = jnp.bfloat16
INDEX_ROW = 5
OFFSET_ROW = 6
BIN_ROW = 16
PACKED_ROWS = 24


def lane_iota(shape):
    return lax.broadcasted_iota(jnp.int32, shape, len(shape) - 1)


def row_iota(shape):
    return lax.broadcasted_iota(jnp.int32, shape, len(shape) - 2)


def near(value):
    return pltpu.with_memory_space_constraint(value, VMEM)


def split(value, count):
    parts = []
    for _ in range(count):
        part = value.astype(BF16)
        parts.append(part)
        value = value - part.astype(F32)
    return parts


def sin_cos_pi(r):
    r2 = r * r
    sine = jnp.zeros_like(r)
    cosine = jnp.zeros_like(r)
    for n in reversed(range(9)):
        sine = sine * r2 + (-1) ** n * math.pi ** (2 * n + 1) / math.factorial(2 * n + 1)
        cosine = cosine * r2 + (-1) ** n * math.pi ** (2 * n) / math.factorial(2 * n)
    return sine * r, cosine


def pack(sft_ref, doppler_ref, antenna_ref, index_ref, offset_ref, out_ref):
    bins = sft_ref.shape[3]
    out_ref[...] = jnp.zeros_like(out_ref)
    for s in range(2):
        out_ref[8 * s : 8 * s + 1, :] = doppler_ref[s : s + 1, :]
        for q in range(2):
            out_ref[8 * s + 1 + 2 * q : 8 * s + 3 + 2 * q, :] = antenna_ref[s, q]
        at = 8 * s + INDEX_ROW
        out_ref[at : at + 1, :] = index_ref[s : s + 1, :].astype(F32)
        at = 8 * s + OFFSET_ROW
        out_ref[at : at + 1, :] = offset_ref[s : s + 1, :].astype(F32)
        for d in range(2):
            at = BIN_ROW + 4 * s + 2 * d
            out_ref[at : at + 2, :bins] = sft_ref[s, d].astype(F32)


def make_taps(wing_ref, packed_ref, out_ref, reach_ref):
    band = lax.axis_index("band")
    last = lax.axis_size("band") - 1
    core = lax.rem(lax.axis_index("seg"), 2)
    beside = jnp.where(core == 0, band - 1, band + 1)
    w_own = wing_ref[band]
    w_beside = wing_ref[jnp.clip(beside, 0, last)]
    w_beside = jnp.where((beside < 0) | (beside > last), 0, w_beside)
    row = row_iota(reach_ref.shape)
    reach = jnp.where((row == 0) & (core == 0) | (row == 2) & (core == 1), w_beside, w_own)
    reach_ref[...] = reach.astype(F32)

    templates = packed_ref.shape[2]
    tap = (WMAX - 1) - row_iota((TAPS, LANES)).astype(F32)
    for seg in range(4):
        side, s = divmod(seg, 2)
        values = packed_ref[side, 8 * s : 8 * s + 5, :]
        table = jnp.concatenate(
            [part.astype(F32) for part in split(values, 3)] + [jnp.zeros((1, templates), F32)], 0
        ).astype(BF16)
        at = 8 * s + INDEX_ROW
        index = packed_ref[side, at : at + 1, :].astype(jnp.int32)
        for tile in range(templates // LANES):
            cols = slice(tile * LANES, (tile + 1) * LANES)
            hot = row_iota((templates, LANES)) == index[:, cols]
            chosen = jnp.dot(table, jnp.where(hot, 1.0, 0.0).astype(BF16), preferred_element_type=F32)
            whole = chosen[0:5] + chosen[5:10] + chosen[10:15]
            shift = whole[0:1]
            sine, cosine = sin_cos_pi(shift - jnp.round(shift))
            factor = sine * (-1.0 / math.pi)
            u = tap - shift
            whole_bin = u == 0
            inverse = 1.0 / u
            real = jnp.where(whole_bin, 1.0, factor * cosine * inverse)
            imag = jnp.where(whole_bin, 0.0, factor * sine * inverse)
            for q in range(2):
                at = (tile * 2 + q) * LANES
                for d in range(2):
                    weight = whole[1 + q * 2 + d : 2 + q * 2 + d]
                    for part, value in enumerate((real, imag)):
                        top = (2 * part + d) * TAPS
                        out_ref[seg, top : top + TAPS, at : at + LANES] = (weight * value).astype(BF16)


def segment_sums(
    scale, packed_ref, halo_ref, reach_ref, taps_ref, out_ref,
    chunk_ref, t_ref, p_ref, u_ref, v_ref, acc_ref
):
    bins = out_ref.shape[2]
    span = bins + 2 * OMAX
    blocks = span // 16
    segs = taps_ref.shape[0]
    core = lax.rem(lax.axis_index("seg"), 2)

    mirror = jnp.where(
        row_iota((LANES, LANES)) + lane_iota((LANES, LANES)) == LANES - 1, 1.0, 0.0
    ).astype(BF16)
    own = [
        jnp.concatenate(
            [packed_ref[side, BIN_ROW:PACKED_ROWS, c * LANES : (c + 1) * LANES] for side in range(2)], 0
        )
        for c in range(2)
    ]
    halo = [
        jnp.concatenate(
            [halo_ref[side, :, c * LANES : (c + 1) * LANES].astype(F32) for side in range(2)], 0
        )
        for c in range(2)
    ]
    first = core == 0
    parts = [
        jnp.where(first, own[1], halo[0]),
        jnp.where(first, own[0], own[1]),
        jnp.where(first, halo[1], own[0]),
    ]
    flipped = jnp.dot(
        jnp.concatenate(parts, 0).astype(BF16), mirror, preferred_element_type=F32
    )
    swapped = pltpu.roll(flipped, HALF, 1)
    for i in range(3):
        chunk_ref[0, i] = flipped[16 * i : 16 * i + 16]
        chunk_ref[1, i] = swapped[16 * i : 16 * i + 16]

    low_half = lane_iota((16, LANES)) < HALF
    within = lane_iota((16, LANES)) % HALF
    bend = within - row_iota((16, LANES))
    center = jnp.abs((WMAX - 0.5) - within.astype(F32))
    reach = [center < reach_ref[i : i + 1, :] for i in range(3)]

    def half_row(h, place, row):
        chunk, half = (h + 1) // 2, (h + 1) % 2
        return jnp.broadcast_to(chunk_ref[half ^ place, chunk, row : row + 1, :], (16, LANES))

    def build(seg):
        for ri in range(2):
            det0, det1 = seg * 4 + ri, seg * 4 + 2 + ri
            for h in range(span // HALF):
                source = jnp.where(low_half, half_row(h, 0, det0), half_row(h, 1, det1))
                after = jnp.where(low_half, half_row(h + 1, 0, det1), half_row(h + 1, 1, det0))
                for a in range(1, 5):
                    turn = LANES - 16 * a
                    window = jnp.where(
                        bend < HALF - 16 * a,
                        pltpu.roll(source, turn, 1, stride=1, stride_axis=0),
                        pltpu.roll(after, turn, 1, stride=1, stride_axis=0),
                    )
                    block = blocks - 4 * h - a
                    side = 0 if block < OMAX // 16 else (2 if block >= blocks - OMAX // 16 else 1)
                    window = jnp.where(reach[side], window, 0.0)
                    same = slice(block * 32 + ri * 16, block * 32 + ri * 16 + 16)
                    other = slice(block * 32 + 16 - ri * 16, block * 32 + 32 - ri * 16)
                    t_ref[seg, same, :LANES] = window.astype(BF16)
                    t_ref[seg, other, LANES:] = (-window if ri else window).astype(BF16)

    def moved(seg, tile, slot):
        at = 8 * (seg % 2) + OFFSET_ROW
        amount = packed_ref[seg // 2, at : at + 1, tile * LANES : (tile + 1) * LANES]
        amount = amount.astype(jnp.int32) + OMAX
        bit = lambda b: jnp.broadcast_to((amount & b) != 0, (8, LANES))
        size = bins // 8
        tiles = [p_ref[slot, 8 * t : 8 * t + 8, :] for t in range(span // 8)]
        far = bit(64)
        tiles = [jnp.where(far, tiles[t + 8], tiles[t]) for t in range(size)] + tiles[size:]
        for b in (32, 16, 8):
            pick, step = bit(b), b // 8
            tiles = [jnp.where(pick, tiles[t + step], tiles[t]) for t in range(size + step)]
        for t, value in enumerate(tiles):
            u_ref[slot, 8 * t : 8 * t + 8, :] = value
        for b, from_ref, to_ref in ((4, u_ref, v_ref), (2, v_ref, u_ref)):
            pick = bit(b)
            for t in range(size + 1):
                end = min(8, bins + b - 8 * t)
                to_ref[slot, 8 * t : 8 * t + end, :] = jnp.where(
                    pick[:end],
                    from_ref[slot, 8 * t + b : 8 * t + b + end, :],
                    from_ref[slot, 8 * t : 8 * t + end, :],
                )
        pick = bit(1)
        return [
            jnp.where(pick, u_ref[slot, 8 * t + 1 : 8 * t + 9, :], u_ref[slot, 8 * t : 8 * t + 8, :])
            for t in range(size)
        ]

    tiles = taps_ref.shape[2] // (2 * LANES)
    each = LANES // out_ref.shape[1]
    build(0)
    for seg in range(segs):
        if seg + 1 < segs:
            build(seg + 1)
        for tile in range(tiles):
            slot = seg * tiles + tile
            amp = jnp.dot(
                t_ref[seg], taps_ref[seg, :, tile * 2 * LANES : (tile + 1) * 2 * LANES],
                preferred_element_type=F32,
            )
            power = (amp * amp).reshape(blocks, 2, 16, 2 * LANES).sum(axis=1)
            power = power.reshape(span, 2 * LANES)
            p_ref[slot] = power[:, :LANES] + power[:, LANES:]
            for t, value in enumerate(moved(seg, tile, slot)):
                if seg == 0:
                    acc_ref[tile, 8 * t : 8 * t + 8, :] = value
                else:
                    acc_ref[tile, 8 * t : 8 * t + 8, :] += value
            if seg == segs - 1:
                turned = (acc_ref[tile] * scale).T.astype(BF16)
                out_ref[tile * each : (tile + 1) * each] = turned.reshape(each, LANES // each, bins)


def per_device(sft, doppler, antenna, coarse_index, freq_offset, wing_width):
    bins = sft.shape[3]
    peers = lax.axis_size("seg")
    count = lax.axis_size("band")
    templates = coarse_index.shape[1]
    fine = templates // peers
    segments = sft.shape[0] * peers
    tiles = templates // LANES
    here = bins // 2
    span = here + 2 * OMAX
    packed = pl.pallas_call(
        pack, out_shape=VMEM((PACKED_ROWS, templates), F32), name="pack"
    )(sft, doppler, antenna, coarse_index, freq_offset)
    pairs = [[i, i + 1] for i in range(0, peers, 2)]
    packed = lax.all_gather(packed[None], "seg", axis=0, tiled=True, axis_index_groups=pairs)
    rows = packed[:, BIN_ROW:, :bins].astype(BF16)
    swap = []
    for low, high in pairs:
        for b in range(1, count):
            swap += [(low * count + b, high * count + b - 1), (high * count + b - 1, low * count + b)]
    halo = lax.ppermute(rows, ("seg", "band"), swap)
    taps, reach = pl.pallas_call(
        make_taps,
        out_shape=(VMEM((4, 4 * TAPS, 2 * templates), BF16), VMEM((8, LANES), F32)),
        in_specs=[pl.BlockSpec(memory_space=pltpu.SMEM), pl.BlockSpec(memory_space=VMEM)],
        name="make_taps",
    )(wing_width, near(packed))
    sent = pl.pallas_call(
        functools.partial(segment_sums, 1.0 / (4 * segments)),
        out_shape=VMEM((peers, fine, here), BF16),
        scratch_shapes=[
            VMEM((2, 3, 16, LANES), F32),
            VMEM((4, 2 * span, 2 * LANES), BF16),
            VMEM((4 * tiles, span, LANES), F32),
            VMEM((4 * tiles, here + 8, LANES), F32),
            VMEM((4 * tiles, here + 8, LANES), F32),
            VMEM((tiles, here, LANES), F32),
        ],
        name="segment_sums",
    )(*[near(z) for z in (packed, halo, reach, taps)])
    recv = lax.all_to_all(sent, "seg", 0, 0, tiled=True)
    halves = jnp.sum(recv.astype(F32).reshape(peers // 2, 2, fine, here), 0)
    return jnp.concatenate([halves[0], halves[1]], 1)


def solution(mesh):
    placed = (
        P("seg", None, None, "band"),
        P("seg", None),
        P("seg", None, None, None),
        P("seg", None),
        P("seg", None),
        P(),
    )
    return jax.shard_map(
        per_device, mesh=mesh, in_specs=placed, out_specs=P("seg", "band"), check_vma=False
    )
```

```python
import functools
import math

import jax
import jax.numpy as jnp
from jax import lax
from jax.experimental import pallas as pl
from jax.experimental.pallas import tpu as pltpu
from jax.sharding import PartitionSpec as P

WMAX = 32
OMAX = 32
LANES = 128
TAPS = 2 * WMAX
HALF = LANES // 2
VMEM = pltpu.VMEM
F32 = jnp.float32
BF16 = jnp.bfloat16
INDEX_ROW = 5
OFFSET_ROW = 6
BIN_ROW = 16
PACKED_ROWS = 24


def lane_iota(shape):
    return lax.broadcasted_iota(jnp.int32, shape, len(shape) - 1)


def row_iota(shape):
    return lax.broadcasted_iota(jnp.int32, shape, len(shape) - 2)


def near(value):
    return pltpu.with_memory_space_constraint(value, VMEM)


def split(value, count):
    parts = []
    for _ in range(count):
        part = value.astype(BF16)
        parts.append(part)
        value = value - part.astype(F32)
    return parts


def sin_cos_pi(r):
    r2 = r * r
    sine = jnp.zeros_like(r)
    cosine = jnp.zeros_like(r)
    for n in reversed(range(9)):
        sine = sine * r2 + (-1) ** n * math.pi ** (2 * n + 1) / math.factorial(2 * n + 1)
        cosine = cosine * r2 + (-1) ** n * math.pi ** (2 * n) / math.factorial(2 * n)
    return sine * r, cosine


def pack(sft_ref, doppler_ref, antenna_ref, index_ref, offset_ref, out_ref):
    bins = sft_ref.shape[3]
    out_ref[...] = jnp.zeros_like(out_ref)
    for s in range(2):
        out_ref[8 * s : 8 * s + 1, :] = doppler_ref[s : s + 1, :]
        for q in range(2):
            out_ref[8 * s + 1 + 2 * q : 8 * s + 3 + 2 * q, :] = antenna_ref[s, q]
        at = 8 * s + INDEX_ROW
        out_ref[at : at + 1, :] = index_ref[s : s + 1, :].astype(F32)
        at = 8 * s + OFFSET_ROW
        out_ref[at : at + 1, :] = offset_ref[s : s + 1, :].astype(F32)
        for d in range(2):
            at = BIN_ROW + 4 * s + 2 * d
            out_ref[at : at + 2, :bins] = sft_ref[s, d].astype(F32)


def mirrored(parts):
    mirror = jnp.where(
        row_iota((LANES, LANES)) + lane_iota((LANES, LANES)) == LANES - 1, 1.0, 0.0
    ).astype(BF16)
    flipped = jnp.dot(jnp.concatenate(parts, 0).astype(BF16), mirror, preferred_element_type=F32)
    swapped = pltpu.roll(flipped, HALF, 1)
    count = parts[0].shape[0]
    cut = lambda value: [value[count * i : count * i + count] for i in range(len(parts))]
    return cut(flipped), cut(swapped)


def own_bins(packed_ref, chunk):
    return jnp.concatenate(
        [packed_ref[side, BIN_ROW:PACKED_ROWS, chunk * LANES : (chunk + 1) * LANES] for side in range(2)], 0
    )


def build_windows(t_ref, chunk_ref, seg, ri, index, last_block, reach):
    low_half = lane_iota((16, LANES)) < HALF
    bend = lane_iota((16, LANES)) % HALF - row_iota((16, LANES))

    def half_row(h, place, row):
        return jnp.broadcast_to(chunk_ref[place, h, row : row + 1, :], (16, LANES))

    det0, det1 = seg * 4 + ri, seg * 4 + 2 + ri
    source = jnp.where(low_half, half_row(index, 0, det0), half_row(index, 1, det1))
    after = jnp.where(low_half, half_row(index + 1, 0, det1), half_row(index + 1, 1, det0))
    for a in range(1, 5):
        turn = LANES - 16 * a
        window = jnp.where(
            bend < HALF - 16 * a,
            pltpu.roll(source, turn, 1, stride=1, stride_axis=0),
            pltpu.roll(after, turn, 1, stride=1, stride_axis=0),
        )
        block = last_block - a
        window = jnp.where(reach[block], window, 0.0)
        same = slice(block * 32 + ri * 16, block * 32 + ri * 16 + 16)
        other = slice(block * 32 + 16 - ri * 16, block * 32 + 32 - ri * 16)
        t_ref[seg, same, :LANES] = window.astype(BF16)
        t_ref[seg, other, LANES:] = (-window if ri else window).astype(BF16)


def power_of(rows, taps):
    amp = jnp.dot(rows, taps, preferred_element_type=F32)
    power = (amp * amp).reshape(rows.shape[0] // 32, 2, 16, 2 * LANES).sum(axis=1)
    power = power.reshape(rows.shape[0] // 2, 2 * LANES)
    return power[:, :LANES] + power[:, LANES:]


def tap_center():
    within = lane_iota((16, LANES)) % HALF
    return jnp.abs((WMAX - 0.5) - within.astype(F32))


def shifted(tiles, packed_ref, seg, tile, u_ref, v_ref):
    at = 8 * (seg % 2) + OFFSET_ROW
    amount = packed_ref[seg // 2, at : at + 1, tile * LANES : (tile + 1) * LANES]
    amount = amount.astype(jnp.int32) + OMAX
    bit = lambda b: jnp.broadcast_to((amount & b) != 0, (8, LANES))
    size = len(tiles) - 8
    rows = 8 * size
    far = bit(64)
    tiles = [jnp.where(far, tiles[t + 8], tiles[t]) for t in range(size)] + tiles[size:]
    for b in (32, 16, 8):
        pick, step = bit(b), b // 8
        tiles = [jnp.where(pick, tiles[t + step], tiles[t]) for t in range(size + step)]
    for t, value in enumerate(tiles):
        u_ref[8 * t : 8 * t + 8, :] = value
    for b, from_ref, to_ref in ((4, u_ref, v_ref), (2, v_ref, u_ref)):
        pick = bit(b)
        for t in range(size + 1):
            end = min(8, rows + b - 8 * t)
            to_ref[8 * t : 8 * t + end, :] = jnp.where(
                pick[:end], from_ref[8 * t + b : 8 * t + b + end, :], from_ref[8 * t : 8 * t + end, :]
            )
    pick = bit(1)
    return [
        jnp.where(pick, u_ref[8 * t + 1 : 8 * t + 9, :], u_ref[8 * t : 8 * t + 8, :])
        for t in range(size)
    ]


def add_tiles(total_ref, tile, values, start):
    for t, value in enumerate(values):
        if start:
            total_ref[tile, 8 * t : 8 * t + 8, :] = value
        else:
            total_ref[tile, 8 * t : 8 * t + 8, :] += value


def inner_power(
    wing_ref, packed_ref, taps_ref, reach_ref, middle_ref, total_ref,
    chunk_ref, t_ref, u_ref, v_ref
):
    band = lax.axis_index("band")
    last = lax.axis_size("band") - 1
    core = lax.rem(lax.axis_index("seg"), 2)
    first = core == 0
    beside = jnp.where(first, band - 1, band + 1)
    w_own = wing_ref[band]
    w_beside = wing_ref[jnp.clip(beside, 0, last)]
    w_beside = jnp.where((beside < 0) | (beside > last), 0, w_beside)
    row = row_iota(reach_ref.shape)
    reach = jnp.where((row == 0) & (core == 0) | (row == 2) & (core == 1), w_beside, w_own)
    reach_ref[...] = reach.astype(F32)

    templates = packed_ref.shape[2]
    tap = (WMAX - 1) - row_iota((TAPS, LANES)).astype(F32)
    for seg in range(4):
        side, s = divmod(seg, 2)
        values = packed_ref[side, 8 * s : 8 * s + 5, :]
        table = jnp.concatenate(
            [part.astype(F32) for part in split(values, 3)] + [jnp.zeros((1, templates), F32)], 0
        ).astype(BF16)
        groups = templates // LANES
        table = jnp.concatenate([table[:, g * LANES : (g + 1) * LANES] for g in range(groups)], 0)
        for tile in range(groups):
            at = 8 * s + INDEX_ROW
            index = packed_ref[side, at : at + 1, tile * LANES : (tile + 1) * LANES].astype(jnp.int32)
            group, place = index // LANES, index % LANES
            hot = jnp.where(row_iota((LANES, LANES)) == place, 1.0, 0.0).astype(BF16)
            found = jnp.dot(table, hot, preferred_element_type=F32)
            chosen = found[:16]
            for g in range(1, groups):
                chosen = jnp.where(group == g, found[16 * g : 16 * g + 16], chosen)
            whole = chosen[0:5] + chosen[5:10] + chosen[10:15]
            shift = whole[0:1]
            sine, cosine = sin_cos_pi(shift - jnp.round(shift))
            factor = sine * (-1.0 / math.pi)
            u = tap - shift
            whole_bin = u == 0
            inverse = 1.0 / u
            real = jnp.where(whole_bin, 1.0, factor * cosine * inverse)
            imag = jnp.where(whole_bin, 0.0, factor * sine * inverse)
            for q in range(2):
                at = (tile * 2 + q) * LANES
                for d in range(2):
                    weight = whole[1 + q * 2 + d : 2 + q * 2 + d]
                    for part, value in enumerate((real, imag)):
                        top = (2 * part + d) * TAPS
                        taps_ref[seg, top : top + TAPS, at : at + LANES] = (weight * value).astype(BF16)

    flipped, swapped = mirrored([own_bins(packed_ref, 1), own_bins(packed_ref, 0)])
    halves = (
        ((swapped[0], flipped[0]), (flipped[0], swapped[0])),
        ((flipped[1], swapped[1]), (swapped[0], flipped[0])),
        ((swapped[1], flipped[1]), (flipped[1], swapped[1])),
    )
    for i, (even, odd) in enumerate(halves):
        for place in range(2):
            chunk_ref[place, i] = jnp.where(first, even[place], odd[place])
    near_reach = [tap_center() < w_own.astype(F32)] * 8
    tiles = templates // LANES
    for seg in range(4):
        for ri in range(2):
            for i in range(2):
                build_windows(t_ref, chunk_ref, seg, ri, i, 8 - 4 * i, near_reach)
        for tile in range(tiles):
            slot = seg * tiles + tile
            power = power_of(
                t_ref[seg], taps_ref[seg, :, tile * 2 * LANES : (tile + 1) * 2 * LANES]
            )
            middle_ref[slot] = jnp.where(first, power[:HALF], power[HALF:])
            parts = [power[8 * t : 8 * t + 8] for t in range(LANES // 8)]
            values = shifted(parts, packed_ref, seg, tile, u_ref.at[slot], v_ref.at[slot])
            add_tiles(total_ref, tile, values, seg == 0)


def segment_sums(
    scale, packed_ref, halo_ref, reach_ref, taps_ref, middle_ref, total_ref, out_ref,
    chunk_ref, t_ref, u_ref, v_ref, acc_ref, *p_refs
):
    bins = out_ref.shape[2]
    segs = taps_ref.shape[0]
    first = lax.rem(lax.axis_index("seg"), 2) == 0
    halo = [
        jnp.concatenate(
            [halo_ref[side, :, c * LANES : (c + 1) * LANES].astype(F32) for side in range(2)], 0
        )
        for c in range(2)
    ]
    parts = [
        jnp.where(first, own_bins(packed_ref, 0), halo[0]),
        jnp.where(first, halo[1], own_bins(packed_ref, 1)),
    ]
    flipped, swapped = mirrored(parts)
    for i, (low, high) in enumerate(((swapped[0], flipped[0]), (flipped[1], swapped[1]))):
        chunk_ref[0, i] = low
        chunk_ref[1, i] = high
    center = tap_center()
    below, above = (center < reach_ref[i : i + 1, :] for i in (0, 2))
    edge_start = pl.multiple_of(jnp.where(first, 0, HALF), 8)
    middle_start = pl.multiple_of(jnp.where(first, HALF, 0), 8)

    tiles = taps_ref.shape[2] // (2 * LANES)
    each = LANES // out_ref.shape[1]
    for seg in range(segs):
        for ri in range(2):
            build_windows(t_ref, chunk_ref, seg, ri, 0, 4, [below, below, above, above])
    for seg in range(segs):
        for tile in range(tiles):
            slot = seg * tiles + tile
            p_refs[slot][pl.ds(middle_start, HALF), :] = middle_ref[slot]
            p_refs[slot][pl.ds(edge_start, HALF), :] = power_of(
                t_ref[seg], taps_ref[seg, :, tile * 2 * LANES : (tile + 1) * 2 * LANES]
            )
            parts = [p_refs[slot][8 * t : 8 * t + 8, :] for t in range(LANES // 8)]
            values = shifted(parts, packed_ref, seg, tile, u_ref.at[slot], v_ref.at[slot])
            add_tiles(acc_ref, tile, values, seg == 0)
            if seg == segs - 1:
                edge, inner = acc_ref[tile], total_ref[tile]
                whole = jnp.concatenate(
                    [jnp.where(first, edge, inner), jnp.where(first, inner, edge)], 0
                )
                turned = (whole * scale).T.astype(BF16)
                out_ref[tile * each : (tile + 1) * each] = turned.reshape(each, LANES // each, bins)


def per_device(sft, doppler, antenna, coarse_index, freq_offset, wing_width):
    bins = sft.shape[3]
    peers = lax.axis_size("seg")
    count = lax.axis_size("band")
    templates = coarse_index.shape[1]
    fine = templates // peers
    segments = sft.shape[0] * peers
    tiles = templates // LANES
    here = bins // 2
    packed = pl.pallas_call(
        pack, out_shape=VMEM((PACKED_ROWS, templates), F32), name="pack"
    )(sft, doppler, antenna, coarse_index, freq_offset)
    pairs = [[i, i + 1] for i in range(0, peers, 2)]
    packed = lax.all_gather(packed[None], "seg", axis=0, tiled=True, axis_index_groups=pairs)
    rows = packed[:, BIN_ROW:, :bins].astype(BF16)
    swap = []
    for low, high in pairs:
        for b in range(1, count):
            swap += [(low * count + b, high * count + b - 1), (high * count + b - 1, low * count + b)]
    halo = lax.ppermute(rows, ("seg", "band"), swap)
    slots = 4 * tiles
    taps, reach, middle, inner = pl.pallas_call(
        inner_power,
        out_shape=(
            VMEM((4, 4 * TAPS, 2 * templates), BF16),
            VMEM((8, LANES), F32),
            VMEM((slots, HALF, LANES), F32),
            VMEM((tiles, HALF, LANES), F32),
        ),
        in_specs=[pl.BlockSpec(memory_space=pltpu.SMEM), pl.BlockSpec(memory_space=VMEM)],
        scratch_shapes=[
            VMEM((2, 3, 16, LANES), F32),
            VMEM((4, 2 * LANES, 2 * LANES), BF16),
            VMEM((slots, HALF + 8, LANES), F32),
            VMEM((slots, HALF + 8, LANES), F32),
        ],
        compiler_params=pltpu.CompilerParams(vmem_limit_bytes=32 << 20),
        name="inner_power",
    )(pltpu.with_memory_space_constraint(wing_width, pltpu.HBM), near(packed))
    sent = pl.pallas_call(
        functools.partial(segment_sums, 1.0 / (4 * segments)),
        out_shape=VMEM((peers, fine, here), BF16),
        scratch_shapes=[
            VMEM((2, 2, 16, LANES), F32),
            VMEM((4, LANES, 2 * LANES), BF16),
            VMEM((slots, HALF + 8, LANES), F32),
            VMEM((slots, HALF + 8, LANES), F32),
            VMEM((tiles, HALF, LANES), F32),
        ] + [VMEM((LANES, LANES), F32)] * slots,
        compiler_params=pltpu.CompilerParams(vmem_limit_bytes=32 << 20),
        name="segment_sums",
    )(*[near(z) for z in (packed, halo, reach, taps, middle, inner)])
    recv = lax.all_to_all(sent, "seg", 0, 0, tiled=True)
    halves = jnp.sum(recv.astype(F32).reshape(peers // 2, 2, fine, here), 0)
    return jnp.concatenate([halves[0], halves[1]], 1)


def solution(mesh):
    placed = (
        P("seg", None, None, "band"),
        P("seg", None),
        P("seg", None, None, None),
        P("seg", None),
        P("seg", None),
        P(),
    )
    return jax.shard_map(
        per_device, mesh=mesh, in_specs=placed, out_specs=P("seg", "band"), check_vma=False
    )
```

```python
import functools
import math

import jax
import jax.numpy as jnp
from jax import lax
from jax.experimental import pallas as pl
from jax.experimental.pallas import tpu as pltpu
from jax.sharding import PartitionSpec as P

WMAX = 32
OMAX = 32
LANES = 128
TAPS = 2 * WMAX
HALF = LANES // 2
VMEM = pltpu.VMEM
F32 = jnp.float32
BF16 = jnp.bfloat16
INDEX_ROW = 5
OFFSET_ROW = 6
BIN_ROW = 16
PACKED_ROWS = 24


def lane_iota(shape):
    return lax.broadcasted_iota(jnp.int32, shape, len(shape) - 1)


def row_iota(shape):
    return lax.broadcasted_iota(jnp.int32, shape, len(shape) - 2)


def near(value):
    return pltpu.with_memory_space_constraint(value, VMEM)


def split(value, count):
    parts = []
    for _ in range(count):
        part = value.astype(BF16)
        parts.append(part)
        value = value - part.astype(F32)
    return parts


def sin_cos_pi(r):
    r2 = r * r
    sine = jnp.zeros_like(r)
    cosine = jnp.zeros_like(r)
    for n in reversed(range(9)):
        sine = sine * r2 + (-1) ** n * math.pi ** (2 * n + 1) / math.factorial(2 * n + 1)
        cosine = cosine * r2 + (-1) ** n * math.pi ** (2 * n) / math.factorial(2 * n)
    return sine * r, cosine


def pack(wing_ref, sft_ref, doppler_ref, antenna_ref, index_ref, offset_ref, out_ref, reach_ref):
    band = lax.axis_index("band")
    last = lax.axis_size("band") - 1
    core = lax.rem(lax.axis_index("seg"), 2)
    beside = jnp.where(core == 0, band - 1, band + 1)
    w_own = wing_ref[band]
    w_beside = wing_ref[jnp.clip(beside, 0, last)]
    w_beside = jnp.where((beside < 0) | (beside > last), 0, w_beside)
    row = row_iota(reach_ref.shape)
    reach = jnp.where((row == 0) & (core == 0) | (row == 2) & (core == 1), w_beside, w_own)
    reach_ref[...] = reach.astype(F32)

    bins = sft_ref.shape[3]
    out_ref[...] = jnp.zeros_like(out_ref)
    for s in range(2):
        out_ref[8 * s : 8 * s + 1, :] = doppler_ref[s : s + 1, :]
        for q in range(2):
            out_ref[8 * s + 1 + 2 * q : 8 * s + 3 + 2 * q, :] = antenna_ref[s, q]
        at = 8 * s + INDEX_ROW
        out_ref[at : at + 1, :] = index_ref[s : s + 1, :].astype(F32)
        at = 8 * s + OFFSET_ROW
        out_ref[at : at + 1, :] = offset_ref[s : s + 1, :].astype(F32)
        for d in range(2):
            at = BIN_ROW + 4 * s + 2 * d
            out_ref[at : at + 2, :bins] = sft_ref[s, d].astype(F32)


def mirrored(parts):
    mirror = jnp.where(
        row_iota((LANES, LANES)) + lane_iota((LANES, LANES)) == LANES - 1, 1.0, 0.0
    ).astype(BF16)
    flipped = jnp.dot(jnp.concatenate(parts, 0).astype(BF16), mirror, preferred_element_type=F32)
    swapped = pltpu.roll(flipped, HALF, 1)
    count = parts[0].shape[0]
    cut = lambda value: [value[count * i : count * i + count] for i in range(len(parts))]
    return cut(flipped), cut(swapped)


def own_bins(packed_ref, chunk):
    return jnp.concatenate(
        [packed_ref[side, BIN_ROW:PACKED_ROWS, chunk * LANES : (chunk + 1) * LANES] for side in range(2)], 0
    )


def build_windows(t_ref, chunk_ref, seg, ri, index, last_block, reach):
    low_half = lane_iota((16, LANES)) < HALF
    bend = lane_iota((16, LANES)) % HALF - row_iota((16, LANES))

    def half_row(h, place, row):
        return jnp.broadcast_to(chunk_ref[place, h, row : row + 1, :], (16, LANES))

    det0, det1 = seg * 4 + ri, seg * 4 + 2 + ri
    source = jnp.where(low_half, half_row(index, 0, det0), half_row(index, 1, det1))
    after = jnp.where(low_half, half_row(index + 1, 0, det1), half_row(index + 1, 1, det0))
    for a in range(1, 5):
        turn = LANES - 16 * a
        window = jnp.where(
            bend < HALF - 16 * a,
            pltpu.roll(source, turn, 1, stride=1, stride_axis=0),
            pltpu.roll(after, turn, 1, stride=1, stride_axis=0),
        )
        block = last_block - a
        window = jnp.where(reach[block], window, 0.0)
        same = slice(block * 32 + ri * 16, block * 32 + ri * 16 + 16)
        other = slice(block * 32 + 16 - ri * 16, block * 32 + 32 - ri * 16)
        t_ref[seg, same, :LANES] = window.astype(BF16)
        t_ref[seg, other, LANES:] = (-window if ri else window).astype(BF16)


def power_of(rows, taps):
    amp = jnp.dot(rows, taps, preferred_element_type=F32)
    power = (amp * amp).reshape(rows.shape[0] // 32, 2, 16, 2 * LANES).sum(axis=1)
    power = power.reshape(rows.shape[0] // 2, 2 * LANES)
    return power[:, :LANES] + power[:, LANES:]


def tap_center():
    within = lane_iota((16, LANES)) % HALF
    return jnp.abs((WMAX - 0.5) - within.astype(F32))


def shifted(tiles, packed_ref, seg, tile, u_ref, v_ref):
    at = 8 * (seg % 2) + OFFSET_ROW
    amount = packed_ref[seg // 2, at : at + 1, tile * LANES : (tile + 1) * LANES]
    amount = amount.astype(jnp.int32) + OMAX
    bit = lambda b: jnp.broadcast_to((amount & b) != 0, (8, LANES))
    size = len(tiles) - 8
    rows = 8 * size
    far = bit(64)
    tiles = [jnp.where(far, tiles[t + 8], tiles[t]) for t in range(size)] + tiles[size:]
    for b in (32, 16, 8):
        pick, step = bit(b), b // 8
        tiles = [jnp.where(pick, tiles[t + step], tiles[t]) for t in range(size + step)]
    for t, value in enumerate(tiles):
        u_ref[8 * t : 8 * t + 8, :] = value
    for b, from_ref, to_ref in ((4, u_ref, v_ref), (2, v_ref, u_ref)):
        pick = bit(b)
        for t in range(size + 1):
            end = min(8, rows + b - 8 * t)
            to_ref[8 * t : 8 * t + end, :] = jnp.where(
                pick[:end], from_ref[8 * t + b : 8 * t + b + end, :], from_ref[8 * t : 8 * t + end, :]
            )
    pick = bit(1)
    return [
        jnp.where(pick, u_ref[8 * t + 1 : 8 * t + 9, :], u_ref[8 * t : 8 * t + 8, :])
        for t in range(size)
    ]


def add_tiles(total_ref, tile, values, start):
    for t, value in enumerate(values):
        if start:
            total_ref[tile, 8 * t : 8 * t + 8, :] = value
        else:
            total_ref[tile, 8 * t : 8 * t + 8, :] += value


def inner_power(
    packed_ref, reach_ref, taps_ref, middle_ref, total_ref,
    chunk_ref, t_ref, u_ref, v_ref
):
    first = lax.rem(lax.axis_index("seg"), 2) == 0
    templates = packed_ref.shape[2]
    tap = (WMAX - 1) - row_iota((TAPS, LANES)).astype(F32)
    for seg in range(4):
        side, s = divmod(seg, 2)
        values = packed_ref[side, 8 * s : 8 * s + 5, :]
        table = jnp.concatenate(
            [part.astype(F32) for part in split(values, 3)] + [jnp.zeros((1, templates), F32)], 0
        ).astype(BF16)
        groups = templates // LANES
        table = jnp.concatenate([table[:, g * LANES : (g + 1) * LANES] for g in range(groups)], 0)
        for tile in range(groups):
            at = 8 * s + INDEX_ROW
            index = packed_ref[side, at : at + 1, tile * LANES : (tile + 1) * LANES].astype(jnp.int32)
            group, place = index // LANES, index % LANES
            hot = jnp.where(row_iota((LANES, LANES)) == place, 1.0, 0.0).astype(BF16)
            found = jnp.dot(table, hot, preferred_element_type=F32)
            chosen = found[:16]
            for g in range(1, groups):
                chosen = jnp.where(group == g, found[16 * g : 16 * g + 16], chosen)
            whole = chosen[0:5] + chosen[5:10] + chosen[10:15]
            shift = whole[0:1]
            sine, cosine = sin_cos_pi(shift - jnp.round(shift))
            factor = sine * (-1.0 / math.pi)
            u = tap - shift
            whole_bin = u == 0
            inverse = 1.0 / u
            real = jnp.where(whole_bin, 1.0, factor * cosine * inverse)
            imag = jnp.where(whole_bin, 0.0, factor * sine * inverse)
            for q in range(2):
                at = (tile * 2 + q) * LANES
                for d in range(2):
                    weight = whole[1 + q * 2 + d : 2 + q * 2 + d]
                    for part, value in enumerate((real, imag)):
                        top = (2 * part + d) * TAPS
                        taps_ref[seg, top : top + TAPS, at : at + LANES] = (weight * value).astype(BF16)

    flipped, swapped = mirrored([own_bins(packed_ref, 1), own_bins(packed_ref, 0)])
    halves = (
        ((swapped[0], flipped[0]), (flipped[0], swapped[0])),
        ((flipped[1], swapped[1]), (swapped[0], flipped[0])),
        ((swapped[1], flipped[1]), (flipped[1], swapped[1])),
    )
    for i, (even, odd) in enumerate(halves):
        for place in range(2):
            chunk_ref[place, i] = jnp.where(first, even[place], odd[place])
    near_reach = [tap_center() < reach_ref[1:2, :]] * 8
    tiles = templates // LANES
    for seg in range(4):
        for ri in range(2):
            for i in range(2):
                build_windows(t_ref, chunk_ref, seg, ri, i, 8 - 4 * i, near_reach)
        for tile in range(tiles):
            slot = seg * tiles + tile
            power = power_of(
                t_ref[seg], taps_ref[seg, :, tile * 2 * LANES : (tile + 1) * 2 * LANES]
            )
            middle_ref[slot] = jnp.where(first, power[:HALF], power[HALF:])
            parts = [power[8 * t : 8 * t + 8] for t in range(LANES // 8)]
            values = shifted(parts, packed_ref, seg, tile, u_ref.at[slot], v_ref.at[slot])
            add_tiles(total_ref, tile, values, seg == 0)


def segment_sums(
    scale, packed_ref, halo_ref, reach_ref, taps_ref, middle_ref, total_ref, out_ref,
    chunk_ref, t_ref, u_ref, v_ref, acc_ref
):
    bins = out_ref.shape[2]
    segs = taps_ref.shape[0]
    first = lax.rem(lax.axis_index("seg"), 2) == 0
    halo = [
        jnp.concatenate(
            [halo_ref[side, :, c * LANES : (c + 1) * LANES].astype(F32) for side in range(2)], 0
        )
        for c in range(2)
    ]
    parts = [
        jnp.where(first, own_bins(packed_ref, 0), halo[0]),
        jnp.where(first, halo[1], own_bins(packed_ref, 1)),
    ]
    flipped, swapped = mirrored(parts)
    for i, (low, high) in enumerate(((swapped[0], flipped[0]), (flipped[1], swapped[1]))):
        chunk_ref[0, i] = low
        chunk_ref[1, i] = high
    center = tap_center()
    below, above = (center < reach_ref[i : i + 1, :] for i in (0, 2))

    tiles = taps_ref.shape[2] // (2 * LANES)
    each = LANES // out_ref.shape[1]
    for seg in range(segs):
        for ri in range(2):
            build_windows(t_ref, chunk_ref, seg, ri, 0, 4, [below, below, above, above])
    for seg in range(segs):
        for tile in range(tiles):
            slot = seg * tiles + tile
            power = power_of(
                t_ref[seg], taps_ref[seg, :, tile * 2 * LANES : (tile + 1) * 2 * LANES]
            )
            middle = middle_ref[slot]
            parts = [jnp.where(first, power, middle), jnp.where(first, middle, power)]
            parts = [part[8 * t : 8 * t + 8] for part in parts for t in range(HALF // 8)]
            values = shifted(parts, packed_ref, seg, tile, u_ref.at[slot], v_ref.at[slot])
            add_tiles(acc_ref, tile, values, seg == 0)
            if seg == segs - 1:
                edge, inner = acc_ref[tile], total_ref[tile]
                whole = jnp.concatenate(
                    [jnp.where(first, edge, inner), jnp.where(first, inner, edge)], 0
                )
                turned = (whole * scale).T.astype(BF16)
                out_ref[tile * each : (tile + 1) * each] = turned.reshape(each, LANES // each, bins)


def per_device(sft, doppler, antenna, coarse_index, freq_offset, wing_width):
    bins = sft.shape[3]
    peers = lax.axis_size("seg")
    count = lax.axis_size("band")
    templates = coarse_index.shape[1]
    fine = templates // peers
    segments = sft.shape[0] * peers
    tiles = templates // LANES
    here = bins // 2
    packed, reach = pl.pallas_call(
        pack,
        out_shape=(VMEM((PACKED_ROWS, templates), F32), VMEM((8, LANES), F32)),
        in_specs=[pl.BlockSpec(memory_space=pltpu.SMEM)] + [pl.BlockSpec(memory_space=VMEM)] * 5,
        name="pack",
    )(wing_width, sft, doppler, antenna, coarse_index, freq_offset)
    pairs = [[i, i + 1] for i in range(0, peers, 2)]
    packed = lax.all_gather(packed[None], "seg", axis=0, tiled=True, axis_index_groups=pairs)
    rows = packed[:, BIN_ROW:, :bins].astype(BF16)
    swap = []
    for low, high in pairs:
        for b in range(1, count):
            swap += [(low * count + b, high * count + b - 1), (high * count + b - 1, low * count + b)]
    halo = lax.ppermute(rows, ("seg", "band"), swap)
    slots = 4 * tiles
    taps, middle, inner = pl.pallas_call(
        inner_power,
        out_shape=(
            VMEM((4, 4 * TAPS, 2 * templates), BF16),
            VMEM((slots, HALF, LANES), F32),
            VMEM((tiles, HALF, LANES), F32),
        ),
        scratch_shapes=[
            VMEM((2, 3, 16, LANES), F32),
            VMEM((4, 2 * LANES, 2 * LANES), BF16),
            VMEM((slots, HALF + 8, LANES), F32),
            VMEM((slots, HALF + 8, LANES), F32),
        ],
        compiler_params=pltpu.CompilerParams(vmem_limit_bytes=32 << 20),
        name="inner_power",
    )(near(packed), near(reach))
    sent = pl.pallas_call(
        functools.partial(segment_sums, 1.0 / (4 * segments)),
        out_shape=VMEM((peers, fine, here), BF16),
        scratch_shapes=[
            VMEM((2, 2, 16, LANES), F32),
            VMEM((4, LANES, 2 * LANES), BF16),
            VMEM((slots, HALF + 8, LANES), F32),
            VMEM((slots, HALF + 8, LANES), F32),
            VMEM((tiles, HALF, LANES), F32),
        ],
        compiler_params=pltpu.CompilerParams(vmem_limit_bytes=32 << 20),
        name="segment_sums",
    )(*[near(z) for z in (packed, halo, reach, taps, middle, inner)])
    recv = lax.all_to_all(sent, "seg", 0, 0, tiled=True)
    halves = jnp.sum(recv.astype(F32).reshape(peers // 2, 2, fine, here), 0)
    return jnp.concatenate([halves[0], halves[1]], 1)


def solution(mesh):
    placed = (
        P("seg", None, None, "band"),
        P("seg", None),
        P("seg", None, None, None),
        P("seg", None),
        P("seg", None),
        P(),
    )
    return jax.shard_map(
        per_device, mesh=mesh, in_specs=placed, out_specs=P("seg", "band"), check_vma=False
    )
```

```python
import functools
import math

import jax
import jax.numpy as jnp
from jax import lax
from jax.experimental import pallas as pl
from jax.experimental.pallas import tpu as pltpu
from jax.sharding import PartitionSpec as P

WMAX = 32
OMAX = 32
LANES = 128
TAPS = 2 * WMAX
HALF = LANES // 2
VMEM = pltpu.VMEM
F32 = jnp.float32
BF16 = jnp.bfloat16
INDEX_ROW = 5
OFFSET_ROW = 6
BIN_ROW = 16
PACKED_ROWS = 24


def lane_iota(shape):
    return lax.broadcasted_iota(jnp.int32, shape, len(shape) - 1)


def row_iota(shape):
    return lax.broadcasted_iota(jnp.int32, shape, len(shape) - 2)


def near(value):
    return pltpu.with_memory_space_constraint(value, VMEM)


def split(value, count):
    parts = []
    for _ in range(count):
        part = value.astype(BF16)
        parts.append(part)
        value = value - part.astype(F32)
    return parts


def sin_cos_pi(r):
    r2 = r * r
    sine = jnp.zeros_like(r)
    cosine = jnp.zeros_like(r)
    for n in reversed(range(9)):
        sine = sine * r2 + (-1) ** n * math.pi ** (2 * n + 1) / math.factorial(2 * n + 1)
        cosine = cosine * r2 + (-1) ** n * math.pi ** (2 * n) / math.factorial(2 * n)
    return sine * r, cosine


def pack(sft_ref, doppler_ref, antenna_ref, index_ref, offset_ref, out_ref):
    bins = sft_ref.shape[3]
    out_ref[...] = jnp.zeros_like(out_ref)
    for s in range(2):
        out_ref[8 * s : 8 * s + 1, :] = doppler_ref[s : s + 1, :]
        for q in range(2):
            out_ref[8 * s + 1 + 2 * q : 8 * s + 3 + 2 * q, :] = antenna_ref[s, q]
        at = 8 * s + INDEX_ROW
        out_ref[at : at + 1, :] = index_ref[s : s + 1, :].astype(F32)
        at = 8 * s + OFFSET_ROW
        out_ref[at : at + 1, :] = offset_ref[s : s + 1, :].astype(F32)
        for d in range(2):
            at = BIN_ROW + 4 * s + 2 * d
            out_ref[at : at + 2, :bins] = sft_ref[s, d].astype(F32)


def mirrored(parts):
    mirror = jnp.where(
        row_iota((LANES, LANES)) + lane_iota((LANES, LANES)) == LANES - 1, 1.0, 0.0
    ).astype(BF16)
    flipped = jnp.dot(jnp.concatenate(parts, 0).astype(BF16), mirror, preferred_element_type=F32)
    swapped = pltpu.roll(flipped, HALF, 1)
    count = parts[0].shape[0]
    cut = lambda value: [value[count * i : count * i + count] for i in range(len(parts))]
    return cut(flipped), cut(swapped)


def own_bins(packed_ref, chunk):
    return jnp.concatenate(
        [packed_ref[side, BIN_ROW:PACKED_ROWS, chunk * LANES : (chunk + 1) * LANES] for side in range(2)], 0
    )


def build_windows(t_ref, chunk_ref, seg, ri, index, last_block, reach):
    low_half = lane_iota((16, LANES)) < HALF
    bend = lane_iota((16, LANES)) % HALF - row_iota((16, LANES))

    def half_row(h, place, row):
        return jnp.broadcast_to(chunk_ref[place, h, row : row + 1, :], (16, LANES))

    det0, det1 = seg * 4 + ri, seg * 4 + 2 + ri
    source = jnp.where(low_half, half_row(index, 0, det0), half_row(index, 1, det1))
    after = jnp.where(low_half, half_row(index + 1, 0, det1), half_row(index + 1, 1, det0))
    for a in range(1, 5):
        turn = LANES - 16 * a
        window = jnp.where(
            bend < HALF - 16 * a,
            pltpu.roll(source, turn, 1, stride=1, stride_axis=0),
            pltpu.roll(after, turn, 1, stride=1, stride_axis=0),
        )
        block = last_block - a
        window = jnp.where(reach[block], window, 0.0)
        same = slice(block * 32 + ri * 16, block * 32 + ri * 16 + 16)
        other = slice(block * 32 + 16 - ri * 16, block * 32 + 32 - ri * 16)
        t_ref[seg, same, :LANES] = window.astype(BF16)
        t_ref[seg, other, LANES:] = (-window if ri else window).astype(BF16)


def power_of(rows, taps):
    amp = jnp.dot(rows, taps, preferred_element_type=F32)
    power = (amp * amp).reshape(rows.shape[0] // 32, 2, 16, 2 * LANES).sum(axis=1)
    power = power.reshape(rows.shape[0] // 2, 2 * LANES)
    return power[:, :LANES] + power[:, LANES:]


def tap_center():
    within = lane_iota((16, LANES)) % HALF
    return jnp.abs((WMAX - 0.5) - within.astype(F32))


def shifted(tiles, packed_ref, seg, tile, u_ref, v_ref):
    at = 8 * (seg % 2) + OFFSET_ROW
    amount = packed_ref[seg // 2, at : at + 1, tile * LANES : (tile + 1) * LANES]
    amount = amount.astype(jnp.int32) + OMAX
    bit = lambda b: jnp.broadcast_to((amount & b) != 0, (8, LANES))
    size = len(tiles) - 8
    rows = 8 * size
    far = bit(64)
    tiles = [jnp.where(far, tiles[t + 8], tiles[t]) for t in range(size)] + tiles[size:]
    for b in (32, 16, 8):
        pick, step = bit(b), b // 8
        tiles = [jnp.where(pick, tiles[t + step], tiles[t]) for t in range(size + step)]
    for t, value in enumerate(tiles):
        u_ref[8 * t : 8 * t + 8, :] = value
    for b, from_ref, to_ref in ((4, u_ref, v_ref), (2, v_ref, u_ref)):
        pick = bit(b)
        for t in range(size + 1):
            end = min(8, rows + b - 8 * t)
            to_ref[8 * t : 8 * t + end, :] = jnp.where(
                pick[:end], from_ref[8 * t + b : 8 * t + b + end, :], from_ref[8 * t : 8 * t + end, :]
            )
    pick = bit(1)
    return [
        jnp.where(pick, u_ref[8 * t + 1 : 8 * t + 9, :], u_ref[8 * t : 8 * t + 8, :])
        for t in range(size)
    ]


def add_tiles(total_ref, tile, values, start):
    for t, value in enumerate(values):
        if start:
            total_ref[tile, 8 * t : 8 * t + 8, :] = value
        else:
            total_ref[tile, 8 * t : 8 * t + 8, :] += value


def inner_power(
    wing_ref, packed_ref, taps_ref, reach_ref, middle_ref, total_ref,
    chunk_ref, t_ref, u_ref, v_ref
):
    band = lax.axis_index("band")
    last = lax.axis_size("band") - 1
    core = lax.rem(lax.axis_index("seg"), 2)
    first = core == 0
    beside = jnp.where(first, band - 1, band + 1)
    w_own = wing_ref[band]
    w_beside = wing_ref[jnp.clip(beside, 0, last)]
    w_beside = jnp.where((beside < 0) | (beside > last), 0, w_beside)
    row = row_iota(reach_ref.shape)
    reach = jnp.where((row == 0) & (core == 0) | (row == 2) & (core == 1), w_beside, w_own)
    reach_ref[...] = reach.astype(F32)

    templates = packed_ref.shape[2]
    tap = (WMAX - 1) - row_iota((TAPS, LANES)).astype(F32)
    for seg in range(4):
        side, s = divmod(seg, 2)
        values = packed_ref[side, 8 * s : 8 * s + 5, :]
        table = jnp.concatenate(
            [part.astype(F32) for part in split(values, 3)] + [jnp.zeros((1, templates), F32)], 0
        ).astype(BF16)
        groups = templates // LANES
        table = jnp.concatenate([table[:, g * LANES : (g + 1) * LANES] for g in range(groups)], 0)
        for tile in range(groups):
            at = 8 * s + INDEX_ROW
            index = packed_ref[side, at : at + 1, tile * LANES : (tile + 1) * LANES].astype(jnp.int32)
            group, place = index // LANES, index % LANES
            hot = jnp.where(row_iota((LANES, LANES)) == place, 1.0, 0.0).astype(BF16)
            found = jnp.dot(table, hot, preferred_element_type=F32)
            chosen = found[:16]
            for g in range(1, groups):
                chosen = jnp.where(group == g, found[16 * g : 16 * g + 16], chosen)
            whole = chosen[0:5] + chosen[5:10] + chosen[10:15]
            shift = whole[0:1]
            sine, cosine = sin_cos_pi(shift - jnp.round(shift))
            factor = sine * (-1.0 / math.pi)
            u = tap - shift
            whole_bin = u == 0
            inverse = 1.0 / u
            real = jnp.where(whole_bin, 1.0, factor * cosine * inverse)
            imag = jnp.where(whole_bin, 0.0, factor * sine * inverse)
            for q in range(2):
                at = (tile * 2 + q) * LANES
                for d in range(2):
                    weight = whole[1 + q * 2 + d : 2 + q * 2 + d]
                    for part, value in enumerate((real, imag)):
                        top = (2 * part + d) * TAPS
                        taps_ref[seg, top : top + TAPS, at : at + LANES] = (weight * value).astype(BF16)

    flipped, swapped = mirrored([own_bins(packed_ref, 1), own_bins(packed_ref, 0)])
    halves = (
        ((swapped[0], flipped[0]), (flipped[0], swapped[0])),
        ((flipped[1], swapped[1]), (swapped[0], flipped[0])),
        ((swapped[1], flipped[1]), (flipped[1], swapped[1])),
    )
    for i, (even, odd) in enumerate(halves):
        for place in range(2):
            chunk_ref[place, i] = jnp.where(first, even[place], odd[place])
    near_reach = [tap_center() < w_own.astype(F32)] * 8
    tiles = templates // LANES
    for seg in range(4):
        for ri in range(2):
            for i in range(2):
                build_windows(t_ref, chunk_ref, seg, ri, i, 8 - 4 * i, near_reach)
        for tile in range(tiles):
            slot = seg * tiles + tile
            power = power_of(
                t_ref[seg], taps_ref[seg, :, tile * 2 * LANES : (tile + 1) * 2 * LANES]
            )
            middle_ref[slot] = jnp.where(first, power[:HALF], power[HALF:])
            parts = [power[8 * t : 8 * t + 8] for t in range(LANES // 8)]
            values = shifted(parts, packed_ref, seg, tile, u_ref.at[slot], v_ref.at[slot])
            add_tiles(total_ref, tile, values, seg == 0)


def segment_sums(
    scale, packed_ref, halo_ref, reach_ref, taps_ref, middle_ref, total_ref, out_ref,
    chunk_ref, t_ref, u_ref, v_ref, acc_ref
):
    bins = out_ref.shape[2]
    segs = taps_ref.shape[0]
    first = lax.rem(lax.axis_index("seg"), 2) == 0
    halo = [
        jnp.concatenate(
            [halo_ref[side, :, c * LANES : (c + 1) * LANES].astype(F32) for side in range(2)], 0
        )
        for c in range(2)
    ]
    parts = [
        jnp.where(first, own_bins(packed_ref, 0), halo[0]),
        jnp.where(first, halo[1], own_bins(packed_ref, 1)),
    ]
    flipped, swapped = mirrored(parts)
    for i, (low, high) in enumerate(((swapped[0], flipped[0]), (flipped[1], swapped[1]))):
        chunk_ref[0, i] = low
        chunk_ref[1, i] = high
    center = tap_center()
    below, above = (center < reach_ref[i : i + 1, :] for i in (0, 2))

    tiles = taps_ref.shape[2] // (2 * LANES)
    each = LANES // out_ref.shape[1]
    for seg in range(segs):
        for ri in range(2):
            build_windows(t_ref, chunk_ref, seg, ri, 0, 4, [below, below, above, above])
    for seg in range(segs):
        for tile in range(tiles):
            slot = seg * tiles + tile
            power = power_of(
                t_ref[seg], taps_ref[seg, :, tile * 2 * LANES : (tile + 1) * 2 * LANES]
            )
            middle = middle_ref[slot]
            parts = [jnp.where(first, power, middle), jnp.where(first, middle, power)]
            parts = [part[8 * t : 8 * t + 8] for part in parts for t in range(HALF // 8)]
            values = shifted(parts, packed_ref, seg, tile, u_ref.at[slot], v_ref.at[slot])
            add_tiles(acc_ref, tile, values, seg == 0)
            if seg == segs - 1:
                edge, inner = acc_ref[tile], total_ref[tile]
                whole = jnp.concatenate(
                    [jnp.where(first, edge, inner), jnp.where(first, inner, edge)], 0
                )
                turned = (whole * scale).T.astype(BF16)
                out_ref[tile * each : (tile + 1) * each] = turned.reshape(each, LANES // each, bins)


def per_device(sft, doppler, antenna, coarse_index, freq_offset, wing_width):
    bins = sft.shape[3]
    peers = lax.axis_size("seg")
    count = lax.axis_size("band")
    templates = coarse_index.shape[1]
    fine = templates // peers
    segments = sft.shape[0] * peers
    tiles = templates // LANES
    here = bins // 2
    packed = pl.pallas_call(
        pack, out_shape=VMEM((PACKED_ROWS, templates), F32), name="pack"
    )(sft, doppler, antenna, coarse_index, freq_offset)
    pairs = [[i, i + 1] for i in range(0, peers, 2)]
    packed = lax.all_gather(packed[None], "seg", axis=0, tiled=True, axis_index_groups=pairs)
    rows = packed[:, BIN_ROW:, :bins].astype(BF16)
    swap = []
    for low, high in pairs:
        for b in range(1, count):
            swap += [(low * count + b, high * count + b - 1), (high * count + b - 1, low * count + b)]
    halo = lax.ppermute(rows, ("seg", "band"), swap)
    slots = 4 * tiles
    taps, reach, middle, inner = pl.pallas_call(
        inner_power,
        out_shape=(
            VMEM((4, 4 * TAPS, 2 * templates), BF16),
            VMEM((8, LANES), F32),
            VMEM((slots, HALF, LANES), F32),
            VMEM((tiles, HALF, LANES), F32),
        ),
        in_specs=[pl.BlockSpec(memory_space=pltpu.SMEM), pl.BlockSpec(memory_space=VMEM)],
        scratch_shapes=[
            VMEM((2, 3, 16, LANES), F32),
            VMEM((4, 2 * LANES, 2 * LANES), BF16),
            VMEM((slots, HALF + 8, LANES), F32),
            VMEM((slots, HALF + 8, LANES), F32),
        ],
        compiler_params=pltpu.CompilerParams(vmem_limit_bytes=32 << 20),
        name="inner_power",
    )(pltpu.with_memory_space_constraint(wing_width, pltpu.HBM), near(packed))
    sent = pl.pallas_call(
        functools.partial(segment_sums, 1.0 / (4 * segments)),
        out_shape=VMEM((peers, fine, here), BF16),
        scratch_shapes=[
            VMEM((2, 2, 16, LANES), F32),
            VMEM((4, LANES, 2 * LANES), BF16),
            VMEM((slots, HALF + 8, LANES), F32),
            VMEM((slots, HALF + 8, LANES), F32),
            VMEM((tiles, HALF, LANES), F32),
        ],
        compiler_params=pltpu.CompilerParams(vmem_limit_bytes=32 << 20),
        name="segment_sums",
    )(*[near(z) for z in (packed, halo, reach, taps, middle, inner)])
    recv = lax.all_to_all(sent, "seg", 0, 0, tiled=True)
    halves = jnp.sum(recv.astype(F32).reshape(peers // 2, 2, fine, here), 0)
    return jnp.concatenate([halves[0], halves[1]], 1)


def solution(mesh):
    placed = (
        P("seg", None, None, "band"),
        P("seg", None),
        P("seg", None, None, None),
        P("seg", None),
        P("seg", None),
        P(),
    )
    return jax.shard_map(
        per_device, mesh=mesh, in_specs=placed, out_specs=P("seg", "band"), check_vma=False
    )
```

```python
import functools
import math

import jax
import jax.numpy as jnp
from jax import lax
from jax.experimental import pallas as pl
from jax.experimental.pallas import tpu as pltpu
from jax.sharding import PartitionSpec as P

WMAX = 32
OMAX = 32
LANES = 128
TAPS = 2 * WMAX
HALF = LANES // 2
VMEM = pltpu.VMEM
F32 = jnp.float32
BF16 = jnp.bfloat16
INDEX_ROW = 5
OFFSET_ROW = 6
BIN_ROW = 16
PACKED_ROWS = 24


def lane_iota(shape):
    return lax.broadcasted_iota(jnp.int32, shape, len(shape) - 1)


def row_iota(shape):
    return lax.broadcasted_iota(jnp.int32, shape, len(shape) - 2)


def near(value):
    return pltpu.with_memory_space_constraint(value, VMEM)


def split(value, count):
    parts = []
    for _ in range(count):
        part = value.astype(BF16)
        parts.append(part)
        value = value - part.astype(F32)
    return parts


def sin_cos_pi(r):
    r2 = r * r
    sine = jnp.zeros_like(r)
    cosine = jnp.zeros_like(r)
    for n in reversed(range(9)):
        sine = sine * r2 + (-1) ** n * math.pi ** (2 * n + 1) / math.factorial(2 * n + 1)
        cosine = cosine * r2 + (-1) ** n * math.pi ** (2 * n) / math.factorial(2 * n)
    return sine * r, cosine


def pack(sft_ref, doppler_ref, antenna_ref, index_ref, offset_ref, out_ref):
    bins = sft_ref.shape[3]
    out_ref[...] = jnp.zeros_like(out_ref)
    for s in range(2):
        out_ref[8 * s : 8 * s + 1, :] = doppler_ref[s : s + 1, :]
        for q in range(2):
            out_ref[8 * s + 1 + 2 * q : 8 * s + 3 + 2 * q, :] = antenna_ref[s, q]
        at = 8 * s + INDEX_ROW
        out_ref[at : at + 1, :] = index_ref[s : s + 1, :].astype(F32)
        at = 8 * s + OFFSET_ROW
        out_ref[at : at + 1, :] = offset_ref[s : s + 1, :].astype(F32)
        for d in range(2):
            at = BIN_ROW + 4 * s + 2 * d
            out_ref[at : at + 2, :bins] = sft_ref[s, d].astype(F32)


def mirrored(parts):
    mirror = jnp.where(
        row_iota((LANES, LANES)) + lane_iota((LANES, LANES)) == LANES - 1, 1.0, 0.0
    ).astype(BF16)
    flipped = jnp.dot(jnp.concatenate(parts, 0).astype(BF16), mirror, preferred_element_type=F32)
    swapped = pltpu.roll(flipped, HALF, 1)
    count = parts[0].shape[0]
    cut = lambda value: [value[count * i : count * i + count] for i in range(len(parts))]
    return cut(flipped), cut(swapped)


def own_bins(packed_ref, chunk):
    return jnp.concatenate(
        [packed_ref[side, BIN_ROW:PACKED_ROWS, chunk * LANES : (chunk + 1) * LANES] for side in range(2)], 0
    )


def build_windows(t_ref, chunk_ref, seg, ri, index, last_block, reach):
    low_half = lane_iota((16, LANES)) < HALF
    bend = lane_iota((16, LANES)) % HALF - row_iota((16, LANES))

    def half_row(h, place, row):
        return jnp.broadcast_to(chunk_ref[place, h, row : row + 1, :], (16, LANES))

    det0, det1 = seg * 4 + ri, seg * 4 + 2 + ri
    source = jnp.where(low_half, half_row(index, 0, det0), half_row(index, 1, det1))
    after = jnp.where(low_half, half_row(index + 1, 0, det1), half_row(index + 1, 1, det0))
    for a in range(1, 5):
        turn = LANES - 16 * a
        window = jnp.where(
            bend < HALF - 16 * a,
            pltpu.roll(source, turn, 1, stride=1, stride_axis=0),
            pltpu.roll(after, turn, 1, stride=1, stride_axis=0),
        )
        block = last_block - a
        window = jnp.where(reach[block], window, 0.0)
        same = slice(block * 32 + ri * 16, block * 32 + ri * 16 + 16)
        other = slice(block * 32 + 16 - ri * 16, block * 32 + 32 - ri * 16)
        t_ref[seg, same, :LANES] = window.astype(BF16)
        t_ref[seg, other, LANES:] = (-window if ri else window).astype(BF16)


def power_of(rows, taps):
    amp = jnp.dot(rows, taps, preferred_element_type=F32)
    power = (amp * amp).reshape(rows.shape[0] // 32, 2, 16, 2 * LANES).sum(axis=1)
    power = power.reshape(rows.shape[0] // 2, 2 * LANES)
    return power[:, :LANES] + power[:, LANES:]


def tap_center():
    within = lane_iota((16, LANES)) % HALF
    return jnp.abs((WMAX - 0.5) - within.astype(F32))


def shifted(tiles, packed_ref, seg, tile, u_ref, v_ref):
    at = 8 * (seg % 2) + OFFSET_ROW
    amount = packed_ref[seg // 2, at : at + 1, tile * LANES : (tile + 1) * LANES]
    amount = amount.astype(jnp.int32) + OMAX
    bit = lambda b: jnp.broadcast_to((amount & b) != 0, (8, LANES))
    size = len(tiles) - 8
    rows = 8 * size
    far = bit(64)
    tiles = [jnp.where(far, tiles[t + 8], tiles[t]) for t in range(size)] + tiles[size:]
    for b in (32, 16, 8):
        pick, step = bit(b), b // 8
        tiles = [jnp.where(pick, tiles[t + step], tiles[t]) for t in range(size + step)]
    for t, value in enumerate(tiles):
        u_ref[8 * t : 8 * t + 8, :] = value
    for b, from_ref, to_ref in ((4, u_ref, v_ref), (2, v_ref, u_ref)):
        pick = bit(b)
        for t in range(size + 1):
            end = min(8, rows + b - 8 * t)
            to_ref[8 * t : 8 * t + end, :] = jnp.where(
                pick[:end], from_ref[8 * t + b : 8 * t + b + end, :], from_ref[8 * t : 8 * t + end, :]
            )
    pick = bit(1)
    return [
        jnp.where(pick, u_ref[8 * t + 1 : 8 * t + 9, :], u_ref[8 * t : 8 * t + 8, :])
        for t in range(size)
    ]


def add_tiles(total_ref, tile, values, start):
    for t, value in enumerate(values):
        if start:
            total_ref[tile, 8 * t : 8 * t + 8, :] = value
        else:
            total_ref[tile, 8 * t : 8 * t + 8, :] += value


def inner_power(
    wing_ref, packed_ref, taps_ref, reach_ref, middle_ref, total_ref,
    chunk_ref, t_ref, u_ref, v_ref
):
    band = lax.axis_index("band")
    last = lax.axis_size("band") - 1
    core = lax.rem(lax.axis_index("seg"), 2)
    first = core == 0
    beside = jnp.where(first, band - 1, band + 1)
    w_own = wing_ref[band]
    w_beside = wing_ref[jnp.clip(beside, 0, last)]
    w_beside = jnp.where((beside < 0) | (beside > last), 0, w_beside)
    row = row_iota(reach_ref.shape)
    reach = jnp.where((row == 0) & (core == 0) | (row == 2) & (core == 1), w_beside, w_own)
    reach_ref[...] = reach.astype(F32)

    templates = packed_ref.shape[2]
    tap = (WMAX - 1) - row_iota((TAPS, LANES)).astype(F32)
    for seg in range(4):
        side, s = divmod(seg, 2)
        values = packed_ref[side, 8 * s : 8 * s + 5, :]
        table = jnp.concatenate(
            [part.astype(F32) for part in split(values, 3)] + [jnp.zeros((1, templates), F32)], 0
        ).astype(BF16)
        groups = templates // LANES
        table = jnp.concatenate([table[:, g * LANES : (g + 1) * LANES] for g in range(groups)], 0)
        for tile in range(groups):
            at = 8 * s + INDEX_ROW
            index = packed_ref[side, at : at + 1, tile * LANES : (tile + 1) * LANES].astype(jnp.int32)
            group, place = index // LANES, index % LANES
            hot = jnp.where(row_iota((LANES, LANES)) == place, 1.0, 0.0).astype(BF16)
            found = jnp.dot(table, hot, preferred_element_type=F32)
            chosen = found[:16]
            for g in range(1, groups):
                chosen = jnp.where(group == g, found[16 * g : 16 * g + 16], chosen)
            whole = chosen[0:5] + chosen[5:10] + chosen[10:15]
            shift = whole[0:1]
            sine, cosine = sin_cos_pi(shift - jnp.round(shift))
            factor = sine * (-1.0 / math.pi)
            u = tap - shift
            whole_bin = u == 0
            inverse = 1.0 / u
            real = jnp.where(whole_bin, 1.0, factor * cosine * inverse)
            imag = jnp.where(whole_bin, 0.0, factor * sine * inverse)
            for q in range(2):
                at = (tile * 2 + q) * LANES
                for d in range(2):
                    weight = whole[1 + q * 2 + d : 2 + q * 2 + d]
                    for part, value in enumerate((real, imag)):
                        top = (2 * part + d) * TAPS
                        taps_ref[seg, top : top + TAPS, at : at + LANES] = (weight * value).astype(BF16)

    flipped, swapped = mirrored([own_bins(packed_ref, 1), own_bins(packed_ref, 0)])
    halves = (
        ((swapped[0], flipped[0]), (flipped[0], swapped[0])),
        ((flipped[1], swapped[1]), (swapped[0], flipped[0])),
        ((swapped[1], flipped[1]), (flipped[1], swapped[1])),
    )
    for i, (even, odd) in enumerate(halves):
        for place in range(2):
            chunk_ref[place, i] = jnp.where(first, even[place], odd[place])
    near_reach = [tap_center() < w_own.astype(F32)] * 8
    tiles = templates // LANES
    for seg in range(4):
        for ri in range(2):
            for i in range(2):
                build_windows(t_ref, chunk_ref, seg, ri, i, 8 - 4 * i, near_reach)
        for tile in range(tiles):
            slot = seg * tiles + tile
            power = power_of(
                t_ref[seg], taps_ref[seg, :, tile * 2 * LANES : (tile + 1) * 2 * LANES]
            )
            middle_ref[slot] = jnp.where(first, power[:HALF], power[HALF:])
            parts = [power[8 * t : 8 * t + 8] for t in range(LANES // 8)]
            values = shifted(parts, packed_ref, seg, tile, u_ref.at[slot], v_ref.at[slot])
            add_tiles(total_ref, tile, values, seg == 0)


def segment_sums(
    scale, packed_ref, halo_ref, reach_ref, taps_ref, middle_ref, total_ref, out_ref,
    chunk_ref, t_ref, u_ref, v_ref, acc_ref, *p_refs
):
    bins = out_ref.shape[2]
    segs = taps_ref.shape[0]
    first = lax.rem(lax.axis_index("seg"), 2) == 0
    halo = jnp.concatenate([halo_ref[side].astype(F32) for side in range(2)], 0)
    parts = [
        jnp.where(first, own_bins(packed_ref, 0), halo),
        jnp.where(first, halo, own_bins(packed_ref, 1)),
    ]
    flipped, swapped = mirrored(parts)
    for i, (low, high) in enumerate(((swapped[0], flipped[0]), (flipped[1], swapped[1]))):
        chunk_ref[0, i] = low
        chunk_ref[1, i] = high
    center = tap_center()
    below, above = (center < reach_ref[i : i + 1, :] for i in (0, 2))
    edge_start = pl.multiple_of(jnp.where(first, 0, HALF), 8)
    middle_start = pl.multiple_of(jnp.where(first, HALF, 0), 8)

    tiles = taps_ref.shape[2] // (2 * LANES)
    each = LANES // out_ref.shape[1]
    for seg in range(segs):
        for ri in range(2):
            build_windows(t_ref, chunk_ref, seg, ri, 0, 4, [below, below, above, above])
    for seg in range(segs):
        for tile in range(tiles):
            slot = seg * tiles + tile
            p_refs[slot][pl.ds(middle_start, HALF), :] = middle_ref[slot]
            p_refs[slot][pl.ds(edge_start, HALF), :] = power_of(
                t_ref[seg], taps_ref[seg, :, tile * 2 * LANES : (tile + 1) * 2 * LANES]
            )
            parts = [p_refs[slot][8 * t : 8 * t + 8, :] for t in range(LANES // 8)]
            values = shifted(parts, packed_ref, seg, tile, u_ref.at[slot], v_ref.at[slot])
            add_tiles(acc_ref, tile, values, seg == 0)
            if seg == segs - 1:
                edge, inner = acc_ref[tile], total_ref[tile]
                whole = jnp.concatenate(
                    [jnp.where(first, edge, inner), jnp.where(first, inner, edge)], 0
                )
                turned = (whole * scale).T.astype(BF16)
                out_ref[tile * each : (tile + 1) * each] = turned.reshape(each, LANES // each, bins)


def per_device(sft, doppler, antenna, coarse_index, freq_offset, wing_width):
    bins = sft.shape[3]
    peers = lax.axis_size("seg")
    count = lax.axis_size("band")
    templates = coarse_index.shape[1]
    fine = templates // peers
    segments = sft.shape[0] * peers
    tiles = templates // LANES
    here = bins // 2
    packed = pl.pallas_call(
        pack, out_shape=VMEM((PACKED_ROWS, templates), F32), name="pack"
    )(sft, doppler, antenna, coarse_index, freq_offset)
    pairs = [[i, i + 1] for i in range(0, peers, 2)]
    packed = lax.all_gather(packed[None], "seg", axis=0, tiled=True, axis_index_groups=pairs)
    even = lax.axis_index("seg") % 2 == 0
    rows = jnp.where(even, packed[:, BIN_ROW:, :LANES], packed[:, BIN_ROW:, bins - LANES : bins])
    rows = rows.astype(BF16)
    swap = []
    for low, high in pairs:
        for b in range(1, count):
            swap += [(low * count + b, high * count + b - 1), (high * count + b - 1, low * count + b)]
    halo = lax.ppermute(rows, ("seg", "band"), swap)
    slots = 4 * tiles
    taps, reach, middle, inner = pl.pallas_call(
        inner_power,
        out_shape=(
            VMEM((4, 4 * TAPS, 2 * templates), BF16),
            VMEM((8, LANES), F32),
            VMEM((slots, HALF, LANES), F32),
            VMEM((tiles, HALF, LANES), F32),
        ),
        in_specs=[pl.BlockSpec(memory_space=pltpu.SMEM), pl.BlockSpec(memory_space=VMEM)],
        scratch_shapes=[
            VMEM((2, 3, 16, LANES), F32),
            VMEM((4, 2 * LANES, 2 * LANES), BF16),
            VMEM((slots, HALF + 8, LANES), F32),
            VMEM((slots, HALF + 8, LANES), F32),
        ],
        compiler_params=pltpu.CompilerParams(vmem_limit_bytes=32 << 20),
        name="inner_power",
    )(pltpu.with_memory_space_constraint(wing_width, pltpu.HBM), near(packed))
    sent = pl.pallas_call(
        functools.partial(segment_sums, 1.0 / (4 * segments)),
        out_shape=VMEM((peers, fine, here), BF16),
        scratch_shapes=[
            VMEM((2, 2, 16, LANES), F32),
            VMEM((4, LANES, 2 * LANES), BF16),
            VMEM((slots, HALF + 8, LANES), F32),
            VMEM((slots, HALF + 8, LANES), F32),
            VMEM((tiles, HALF, LANES), F32),
        ] + [VMEM((LANES, LANES), F32)] * slots,
        compiler_params=pltpu.CompilerParams(vmem_limit_bytes=32 << 20),
        name="segment_sums",
    )(*[near(z) for z in (packed, halo, reach, taps, middle, inner)])
    recv = lax.all_to_all(sent, "seg", 0, 0, tiled=True)
    halves = jnp.sum(recv.astype(F32).reshape(peers // 2, 2, fine, here), 0)
    return jnp.concatenate([halves[0], halves[1]], 1)


def solution(mesh):
    placed = (
        P("seg", None, None, "band"),
        P("seg", None),
        P("seg", None, None, None),
        P("seg", None),
        P("seg", None),
        P(),
    )
    return jax.shard_map(
        per_device, mesh=mesh, in_specs=placed, out_specs=P("seg", "band"), check_vma=False
    )
```
